128 devices in a mesh: stars: 32 (over z, x, core), seg: 4 (over y).
Axes of the slice: x: 4, y: 4, z: 4, core: 2. Of those that a mesh axis runs over, the one named last changes fastest.
Arguments:
- obs_star: int32 [16384, 128], P(('stars', 'seg')), may hold values from 0 to 8191
- obs_knot: int32 [16384, 128], P(('stars', 'seg')), may hold values from 0 to 8191
- obs_frac: float32 [16384, 128], P(('stars', 'seg')), may hold values from 0 to 1
- star_coef: float32 [5, 16384, 128], P(None, ('stars', 'seg')), may hold values from -6 to 6
- att_coef: float32 [4, 16384, 128], P(None, ('stars', 'seg')), may hold values from -3 to 3
- cal_coef: float32 [16384, 128], P(('stars', 'seg')), may hold values from -6 to 6
- tile_cal: int32 [16384], P(('stars', 'seg')), may hold values from 0 to 255
- live_tiles: int32 [128], P(('stars', 'seg')), may hold values from 1 to 128, as said below
- obs_value: float32 [16384, 128], P(('stars', 'seg')), may hold values from -8 to 8
Outputs:
- star_solution: float32 [5, 262144], P(None, 'stars')
- attitude_solution: float32 [4, 32768], P(None, 'seg')
- calibration_solution: float32 [1024, 128], P('seg')
- residual: float32 [16384, 128], P(('stars', 'seg'))
The draws below stay inside these ranges and needn't reach their ends.
Inputs may be any that keep to these rules, and one draw needn't show every extreme that they name: Entry d belongs to device d in the order of the stars axis, then seg; that device's first live_tiles[d] tile slots are live and the rest are padding; some device has all 128 slots live. `obs_knot`: knots past a segment's last knot are the next segment's first knots.
All inputs are finite; a program needn't handle non-finite values.
Results may differ from the reference program's by a relative error of at most 0.00017.
Values sent between devices are 32-bit elements; how exact they have to be, the bound alone decides.
A program may use at most 128 MiB of HBM per device.

```python
import jax
import jax.numpy as jnp

STAR_DEV = 8192
KNOT_DEV = 8192
CALB_DEV = 256
TILE_DEV = 128
TILE_OBS = 128
ITERS = 2
NSTARS = 262144
NKNOTS = 32768
NCALB = 1024
NTILES = 16384
N_STARS = 32
N_SEG = 4
DEVICES = 128


def draw_live_tiles(key, part):
    load_key, jitter_key, chosen_key = jax.random.split(key, 3)
    seg_load = jax.random.randint(load_key, (N_SEG,), 1, 5)
    jitter = jax.random.randint(jitter_key, (DEVICES,), 0, TILE_DEV // 8 + 1)
    device = jnp.arange(DEVICES, dtype=jnp.int32)
    counts = jnp.maximum(TILE_DEV * seg_load[device % N_SEG] // 4 - jitter, 1)
    chosen = jax.random.randint(chosen_key, (), 0, DEVICES)
    return jnp.where(device == chosen, TILE_DEV, counts).astype(jnp.int32)


def draw_obs_value(key, part):
    noise_key = jax.random.fold_in(key, 0)
    rows = jnp.arange(NTILES, dtype=jnp.int32)
    block_pos = (rows // (TILE_DEV * N_SEG)).astype(jnp.float32)
    scale = 0.5 + 1.5 * block_pos / max(N_STARS - 1, 1)
    noise = jnp.clip(jax.random.normal(noise_key, (NTILES, TILE_OBS), jnp.float32), -4.0, 4.0)
    return (noise * scale[:, None]).astype(jnp.float32)


def set_ends(array, rng, low, high):
    spot = [jax.random.randint(jax.random.fold_in(rng, axis), (), 0, length) for axis, length in enumerate(array.shape)]
    widest = array.shape.index(max(array.shape))
    neighbour = spot[:widest] + [(spot[widest] + 1) % array.shape[widest]] + spot[widest + 1:]
    return array.at[tuple(spot)].set(low).at[tuple(neighbour)].set(high)


def level_of(stream_key, dims, cuts, smallest, high):
    loudness, own = 1.0, jax.random.fold_in(stream_key, 6)
    for position, shards_of in cuts:
        heights = jnp.exp(jax.random.uniform(jax.random.fold_in(own, position), (shards_of,), jnp.float32, smallest / len(cuts), high / len(cuts)))
        loudness = loudness * jnp.repeat(heights, dims[position] // shards_of).reshape([-1 if axis == position else 1 for axis in range(len(dims))])
    return loudness


def normal_values(key, dims, scale, limit, cuts=(), kind=jnp.bfloat16):
    values = scale * jax.random.normal(key, dims, jnp.float32)
    if cuts:
        values = values * level_of(key, dims, cuts, -0.22, 0.18)
    return jnp.clip(values, -limit, limit).astype(kind)


def setup_inputs(seed: int = 0) -> dict:
    key_of = jax.random.split(jax.random.key(seed), 10)
    return {
        "obs_star": set_ends(jax.random.randint(key_of[0], (NTILES, TILE_OBS), 0, STAR_DEV), jax.random.fold_in(key_of[0], 1), 0, STAR_DEV - 1).astype(jnp.int32),
        "obs_knot": set_ends(jax.random.randint(key_of[1], (NTILES, TILE_OBS), 0, KNOT_DEV), jax.random.fold_in(key_of[1], 1), 0, KNOT_DEV - 1).astype(jnp.int32),
        "obs_frac": jnp.clip(1.0 * jax.random.uniform(key_of[2], (NTILES, TILE_OBS), jnp.float32) ** level_of(key_of[2], (NTILES, TILE_OBS), ((0, 128),), -0.2, 0.2), 0.0, 1.0),
        "star_coef": normal_values(key_of[3], (5, NTILES, TILE_OBS), 1.0, 6.0, ((1, 128),), jnp.float32),
        "att_coef": normal_values(key_of[4], (4, NTILES, TILE_OBS), 0.5, 3.0, ((1, 128),), jnp.float32),
        "cal_coef": normal_values(key_of[5], (NTILES, TILE_OBS), 1.0, 6.0, ((0, 128),), jnp.float32),
        "tile_cal": set_ends(jax.random.randint(key_of[6], (NTILES,), 0, CALB_DEV), jax.random.fold_in(key_of[6], 1), 0, CALB_DEV - 1).astype(jnp.int32),
        "live_tiles": draw_live_tiles(jax.random.fold_in(key_of[9], 71), 0),
        "obs_value": draw_obs_value(jax.random.fold_in(key_of[9], 71), 0),
    }


def spline_weights(fraction):
    remain = 1.0 - fraction
    square = fraction * fraction
    cubed = square * fraction
    return (remain * remain * remain / 6.0,
            (3.0 * cubed - 6.0 * square + 4.0) / 6.0,
            (-3.0 * cubed + 3.0 * square + 3.0 * fraction + 1.0) / 6.0,
            cubed / 6.0)


def reference(obs_star, obs_knot, obs_frac, star_coef, att_coef, cal_coef, tile_cal, live_tiles, obs_value):
    tile_ids = jnp.arange(NTILES, dtype=jnp.int32)
    device = tile_ids // TILE_DEV
    block_ids = device // N_SEG
    segment = device % N_SEG
    live_mask = ((tile_ids % TILE_DEV) < live_tiles[device]).astype(jnp.float32)[:, None]
    star_ids = obs_star + (block_ids * STAR_DEV)[:, None]
    knot_ids = obs_knot + (segment * KNOT_DEV)[:, None]
    cal_rows = tile_cal + segment * CALB_DEV
    weights = spline_weights(obs_frac)

    def forward(star_x, att_x, cal_x):
        padded = jnp.concatenate([att_x, jnp.zeros((4, 3), jnp.float32)], axis=1)
        result = jnp.zeros((NTILES, TILE_OBS), jnp.float32)
        for comp in range(5):
            result = result + star_coef[comp] * star_x[comp][star_ids]
        for offset in range(4):
            for comp in range(4):
                result = result + weights[offset] * att_coef[comp] * padded[comp][knot_ids + offset]
        result = result + cal_coef * cal_x[cal_rows]
        return result * live_mask

    def backward(values):
        masked = values * live_mask
        flat_stars = star_ids.ravel()
        star_grad = jnp.stack([jax.ops.segment_sum((star_coef[comp] * masked).ravel(), flat_stars, num_segments=NSTARS) for comp in range(5)])
        att_rows = []
        for comp in range(4):
            acc = jnp.zeros((NKNOTS + 3,), jnp.float32)
            for offset in range(4):
                acc = acc + jax.ops.segment_sum((att_coef[comp] * weights[offset] * masked).ravel(), (knot_ids + offset).ravel(), num_segments=NKNOTS + 3)
            att_rows.append(acc[:NKNOTS])
        att_grad = jnp.stack(att_rows)
        cal_grad = jax.ops.segment_sum(cal_coef * masked, cal_rows, num_segments=NCALB)
        return (star_grad, att_grad, cal_grad)

    def squares(parts):
        return sum(jnp.sum(piece * piece) for piece in parts)

    residual = obs_value * live_mask
    gradient = backward(residual)
    grad_norm = squares(gradient)
    direction = gradient
    solution = tuple(jnp.zeros_like(piece) for piece in gradient)
    for iteration in range(ITERS):
        image = forward(*direction)
        step_size = grad_norm / jnp.sum(image * image)
        solution = tuple(current + step_size * moving for current, moving in zip(solution, direction))
        residual = residual - step_size * image
        gradient = backward(residual)
        new_norm = squares(gradient)
        direction = tuple(fresh + (new_norm / grad_norm) * moving for fresh, moving in zip(gradient, direction))
        grad_norm = new_norm
    return (solution[0], solution[1], solution[2], residual)
```

```python
import functools
import jax, jax.numpy as jnp
from jax import lax
from jax.experimental import pallas as pl
from jax.experimental.pallas import tpu as pltpu
BF=jnp.bfloat16; F32=jnp.float32
SE=40

def iota16():
    return lax.broadcasted_iota(jnp.int32,(16,128),0).astype(F32).astype(BF)

def row16(ref, t):
    return jnp.broadcast_to(ref[pl.ds(t,1),:],(16,128)).astype(BF)

def onehot(ref, t, n):
    r=row16(ref,t); i=iota16()
    one=jnp.ones((16,128),BF); zero=jnp.zeros((16,128),BF)
    return jnp.concatenate([jnp.where(i+BF(16*k)==r,one,zero) for k in range(n//16)],axis=0)

def split(x):
    hi=x.astype(BF); lo=(x-hi.astype(F32)).astype(BF)
    return hi,lo

def prep(star_ref, knot_ref, frac_ref, ms, ss, ma, w_ref):
    s=star_ref[...]; k=knot_ref[...]
    ms[...]=(s&255).astype(F32); ss[...]=(s>>8).astype(F32)
    ma[...]=(k>>5).astype(F32)
    def body(t,_):
        u=jnp.broadcast_to(frac_ref[pl.ds(t,1),:],(8,128))
        kk=jnp.broadcast_to(knot_ref[pl.ds(t,1),:]&31,(8,128))
        rem=1.0-u; sq=u*u; cu=sq*u
        w=(rem*rem*rem/6.0,(3.0*cu-6.0*sq+4.0)/6.0,(-3.0*cu+3.0*sq+3.0*u+1.0)/6.0,cu/6.0)
        i8=lax.broadcasted_iota(jnp.int32,(8,128),0)
        for j in range(SE//8):
            d=i8+8*j-kk
            v=jnp.where(d==0,w[0],jnp.where(d==1,w[1],jnp.where(d==2,w[2],jnp.where(d==3,w[3],0.0))))
            w_ref[t,pl.ds(8*j,8),:]=v
        return 0
    lax.fori_loop(0,128,body,0)

def bwd(r_val, sc_ref, ac_ref, cc_ref, caln_ref, ms, ss, ma, w_ref, pst, pat, pstl, accs, acca, cal_out, U):
    for c in range(5):
        p=sc_ref[c]*r_val
        hi=p.astype(BF).astype(F32)
        pst[c]=hi; pstl[c]=p-hi
    for q in range(4):
        pat[q]=ac_ref[q]*r_val
    pc=cc_ref[...]*r_val
    hi,lo=split(pc)
    icl=lax.broadcasted_iota(jnp.int32,(256,128),0)
    hc=jnp.where(icl==jnp.broadcast_to(caln_ref[...],(256,128)),1.0,0.0).astype(BF)
    cal_out[...]=jnp.dot(hc,hi,preferred_element_type=F32)+jnp.dot(hc,lo,preferred_element_type=F32)
    accs[...]=jnp.zeros_like(accs); acca[...]=jnp.zeros_like(acca)
    z16=jnp.zeros((16,128),BF)
    def body(b,_):
        Hs=[];Ha=[];As=[];Aa=[]
        for u in range(U):
            t=b*U+u
            Hs.append(onehot(ms,t,256)); Ha.append(onehot(ma,t,256))
            r=row16(ss,t); i=iota16()
            mk=[(i+BF(16*k))==r for k in range(2)]
            his=[];los=[]
            for c in range(5):
                h=row16(pst.at[c],t); l=row16(pstl.at[c],t)
                his+= [jnp.where(m,h,z16) for m in mk]
                los+= [jnp.where(m,l,z16) for m in mk]
            As.append(jnp.concatenate(his+los,axis=0))
            W=w_ref[t]
            hs=[];ls=[]
            for q in range(4):
                a=W*jnp.broadcast_to(pat[q,pl.ds(t,1),:],(SE,128))
                hs.append(a)
            a=jnp.concatenate(hs,axis=0)
            h,l=split(a)
            Aa.append(jnp.concatenate([h,l],axis=0))
        dn=(((1,),(1,)),((),()))
        accs[...]+=lax.dot_general(jnp.concatenate(As,1),jnp.concatenate(Hs,1),dn,preferred_element_type=F32)
        acca[...]+=lax.dot_general(jnp.concatenate(Aa,1),jnp.concatenate(Ha,1),dn,preferred_element_type=F32)
        return 0
    lax.fori_loop(0,128//U,body,0)

def fwd(xs_ref, xa_ref, sc_ref, ac_ref, ms, ss, ma, w_ref, out_ref, U):
    i8=lax.broadcasted_iota(jnp.int32,(8,128),0).astype(F32)
    def body(b,_):
        Hs=[onehot(ms,b*U+u,256) for u in range(U)]
        Ts=jnp.dot(xs_ref[...],jnp.concatenate(Hs,1),preferred_element_type=F32)
        Ha=[onehot(ma,b*U+u,256) for u in range(U)]
        Ta=jnp.dot(xa_ref[...],jnp.concatenate(Ha,1),preferred_element_type=F32)
        rows=[]
        for u in range(U):
            t=b*U+u
            sl=slice(128*u,128*u+128)
            g=None
            for c in range(5):
                x=(Ts[32*c:32*c+32,sl]+Ts[160+32*c:192+32*c,sl])*jnp.broadcast_to(sc_ref[c,pl.ds(t,1),:],(32,128))
                g=x if g is None else g+x
            s=jnp.broadcast_to(ss[pl.ds(t,1),:],(8,128))
            tot=None
            for j in range(4):
                x=jnp.where(i8+8.0*j==s,g[8*j:8*j+8],0.0)
                tot=x if tot is None else tot+x
            g=None
            for q in range(4):
                x=(Ta[SE*q:SE*q+SE,sl]+Ta[4*SE+SE*q:4*SE+SE*q+SE,sl])*jnp.broadcast_to(ac_ref[q,pl.ds(t,1),:],(SE,128))
                g=x if g is None else g+x
            g=g*w_ref[t]
            for j in range(SE//8):
                tot=tot+g[8*j:8*j+8]
            rows.append(jnp.sum(tot,axis=0,keepdims=True))
        out_ref[pl.ds(b*U,U),:]=jnp.concatenate(rows,0)
        return 0
    lax.fori_loop(0,128//U,body,0)

VM = pl.BlockSpec(memory_space=pltpu.VMEM)
S = jax.ShapeDtypeStruct
TT = (128, 128)

def k_prep(star, knot, frac):
    def kern(a, b, c, ms, ss, ma, w):
        prep(a, b, c, ms, ss, ma, w)
    return pl.pallas_call(kern, in_specs=[VM]*3, out_specs=[VM]*4,
        out_shape=[S(TT,F32)]*3+[S((128,SE,128),F32)], name="prep")(star, knot, frac)

def k_bwd(r, sc, ac, cc, caln, ms, ss, ma, w):
    def kern(r, sc, ac, cc, caln, ms, ss, ma, w, os, oa, oc, pst, pstl, pat, accs, acca):
        bwd(r[...], sc, ac, cc, caln, ms, ss, ma, w, pst, pat, pstl, accs, acca, oc, 8)
        os[...] = accs[0:160] + accs[160:320]
        oa[...] = acca[0:160] + acca[160:320]
    return pl.pallas_call(kern, in_specs=[VM]*9, out_specs=[VM]*3,
        out_shape=[S((160,256),F32),S((160,256),F32),S((256,128),F32)],
        scratch_shapes=[pltpu.VMEM((5,128,128),F32)]*2+[pltpu.VMEM((4,128,128),F32)]+[pltpu.VMEM((320,256),F32)]*2,
        name="bwd", compiler_params=pltpu.CompilerParams(vmem_limit_bytes=50<<20))(r, sc, ac, cc, caln, ms, ss, ma, w)

def k_fwd(xs, xa, xc, sc, ac, cc, calt, mask, ms, ss, ma, w):
    def kern(xs, xa, xc, sc, ac, cc, calt, mask, ms, ss, ma, w, out, bxs, bxa):
        for x, bx in ((xs, bxs), (xa, bxa)):
            h, l = split(x[...])
            bx[0:160] = h
            bx[160:320] = l
        fwd(bxs, bxa, sc, ac, ms, ss, ma, w, out, 8)
        icl = lax.broadcasted_iota(jnp.int32, (128, 256), 1)
        hc = jnp.where(icl == jnp.broadcast_to(calt[...], (128, 256)), 1.0, 0.0).astype(BF)
        h, l = split(xc[...])
        v = jnp.dot(hc, h, preferred_element_type=F32) + jnp.dot(hc, l, preferred_element_type=F32)
        out[...] = (out[...] + cc[...] * v) * mask[...]
    return pl.pallas_call(kern, in_specs=[VM]*12, out_specs=VM, out_shape=S(TT,F32),
        scratch_shapes=[pltpu.VMEM((320,256),BF)]*2, name="fwd",
        compiler_params=pltpu.CompilerParams(vmem_limit_bytes=50<<20))(xs, xa, xc, sc, ac, cc, calt, mask, ms, ss, ma, w)

def shifted(block, axis, distance):
    devices = range(lax.axis_size(axis))
    route = [(i - distance, i) for i in devices if i - distance in devices]
    return lax.ppermute(block, axis, route)

def on_device(star, knot, frac, sc, ac, cc, tile_cal, live, obs):
    mask = jnp.broadcast_to((jnp.arange(128, dtype=jnp.int32) < live[0]).astype(F32)[:, None], TT)
    ms, ss, ma, w = k_prep(star, knot, frac)
    caln = tile_cal.reshape(1, 128)
    calt = tile_cal.reshape(128, 1)

    def gradient(r):
        gs, ga, gc = k_bwd(r, sc, ac, cc, caln, ms, ss, ma, w)
        ga = ga.reshape(4, SE, 256)
        spill = ga[:, 32:35]
        behind = shifted(spill[:, :, 255:], "seg", 1)
        ga = ga[:, :32].at[:, :3].add(jnp.concatenate([behind, spill[:, :, :255]], axis=2))
        ga, gc = lax.psum((ga, gc), "stars")
        gs = lax.psum(gs, "seg")
        return gs, ga, gc

    def forward(d):
        xs, xa, xc = d
        ahead = shifted(xa[:, :3, :1], "seg", -1)
        ext = jnp.concatenate([xa[:, :3, 1:], ahead], axis=2)
        xe = jnp.concatenate([xa, ext, jnp.zeros((4, SE - 35, 256), F32)], axis=1).reshape(4 * SE, 256)
        return k_fwd(xs, xe, xc, sc, ac, cc, calt, mask, ms, ss, ma, w)

    def total(x):
        return lax.psum(x, ("stars", "seg"))

    def sq(p):
        return jnp.sum(p[0] * p[0]) / 4 + (jnp.sum(p[1] * p[1]) + jnp.sum(p[2] * p[2])) / 32

    r = obs * mask
    g = gradient(r)
    gg = total(sq(g))
    d = g
    sol = None
    for it in range(2):
        q = forward(d)
        alpha = gg / total(jnp.sum(q * q))
        r = r - alpha * q
        sol = tuple(alpha * a for a in d) if sol is None else tuple(s + alpha * a for s, a in zip(sol, d))
        if it == 0:
            g = gradient(r)
            new = total(sq(g))
            d = tuple(a + (new / gg) * b for a, b in zip(g, d))
            gg = new
    xs = sol[0].reshape(5, 8192)
    xa = jnp.swapaxes(sol[1], 1, 2).reshape(4, 8192)
    return xs, xa, sol[2], r

def solution(mesh):
    P = jax.sharding.PartitionSpec
    a = P(("stars", "seg"), None)
    b = P(None, ("stars", "seg"), None)
    c = P(("stars", "seg"))
    return jax.shard_map(on_device, mesh=mesh, in_specs=(a, a, a, b, b, a, c, c, a),
        out_specs=(P(None, "stars"), P(None, "seg"), P("seg", None), a), check_vma=False)
```

```python
import jax
import jax.numpy as jnp
from jax import lax
from jax.experimental import pallas as pl
from jax.experimental.pallas import tpu as pltpu

BF = jnp.bfloat16
F32 = jnp.float32
SE = 40
U = 8
LOOPS = 128 // U
NS = 32
NG = 4
MESH = pl.DeviceIdType.MESH


def split(x):
    hi = x.astype(BF)
    return hi, (x - hi.astype(F32)).astype(BF)


def row16(ref, t):
    return jnp.broadcast_to(ref[pl.ds(t, 1), :], (16, 128)).astype(BF)


def iota16():
    return lax.broadcasted_iota(jnp.int32, (16, 128), 0).astype(F32).astype(BF)


def onehot(ref, t, n):
    r = row16(ref, t)
    i = iota16()
    one = jnp.ones((16, 128), BF)
    zero = jnp.zeros((16, 128), BF)
    return jnp.concatenate([jnp.where(i + BF(16 * k) == r, one, zero) for k in range(n // 16)], axis=0)


def iota(shape, axis):
    return lax.broadcasted_iota(jnp.int32, shape, axis)


def prepare(star, knot, frac, ms, ss, ma, sa, wk, w_tab):
    s = star[...]
    k = knot[...]
    ms[...] = (s & 255).astype(F32)
    ss[...] = (s >> 8).astype(F32)
    ma[...] = (k >> 5).astype(F32)
    sa[...] = k & 31
    u = frac[...]
    rem = 1.0 - u
    sq = u * u
    cu = sq * u
    wk[0] = rem * rem * rem / 6.0
    wk[1] = (3.0 * cu - 6.0 * sq + 4.0) / 6.0
    wk[2] = (-3.0 * cu + 3.0 * sq + 3.0 * u + 1.0) / 6.0
    wk[3] = cu / 6.0

    def body(t, _):
        kk = jnp.broadcast_to(sa[pl.ds(t, 1), :], (8, 128))
        w = [jnp.broadcast_to(wk[j, pl.ds(t, 1), :], (8, 128)) for j in range(4)]
        base = iota((8, 128), 0) - kk
        for j in range(SE // 8):
            d = base + 8 * j
            v = jnp.where(d == 0, w[0], jnp.where(d == 1, w[1], jnp.where(d == 2, w[2], jnp.where(d == 3, w[3], 0.0))))
            w_tab[t, pl.ds(8 * j, 8), :] = v
        return 0

    lax.fori_loop(0, 128, body, 0)


DN = (((1,), (1,)), ((), ()))


def back_att(start, stop, pat, ma, w_tab, acc):
    def body(b, _):
        hs = []
        rows = []
        for u in range(U):
            t = b * U + u
            hs.append(onehot(ma, t, 256))
            w = w_tab[t]
            a = jnp.concatenate([w * jnp.broadcast_to(pat[q, pl.ds(t, 1), :], (SE, 128)) for q in range(4)], axis=0)
            h, l = split(a)
            rows.append(jnp.concatenate([h, l], axis=0))
        acc[...] += lax.dot_general(jnp.concatenate(rows, 1), jnp.concatenate(hs, 1), DN, preferred_element_type=F32)
        return 0

    lax.fori_loop(start, stop, body, 0)


def back_star(start, stop, psh, psl, ms, ss, acc):
    z16 = jnp.zeros((16, 128), BF)

    def body(b, _):
        hs = []
        rows = []
        for u in range(U):
            t = b * U + u
            hs.append(onehot(ms, t, 256))
            r = row16(ss, t)
            i = iota16()
            masks = [(i + BF(16 * k)) == r for k in range(2)]
            his = []
            los = []
            for c in range(5):
                h = row16(psh.at[c], t)
                l = row16(psl.at[c], t)
                his += [jnp.where(m, h, z16) for m in masks]
                los += [jnp.where(m, l, z16) for m in masks]
            rows.append(jnp.concatenate(his + los, axis=0))
        acc[...] += lax.dot_general(jnp.concatenate(rows, 1), jnp.concatenate(hs, 1), DN, preferred_element_type=F32)
        return 0

    lax.fori_loop(start, stop, body, 0)


def fwd_star(tab, sc, ms, ss, out):
    i8 = iota((8, 128), 0).astype(F32)

    def body(b, _):
        h = jnp.concatenate([onehot(ms, b * U + u, 256) for u in range(U)], 1)
        x = jnp.dot(tab[...], h, preferred_element_type=F32)
        rows = []
        for u in range(U):
            t = b * U + u
            sl = slice(128 * u, 128 * u + 128)
            g = None
            for c in range(5):
                y = (x[32 * c:32 * c + 32, sl] + x[160 + 32 * c:192 + 32 * c, sl]) * jnp.broadcast_to(sc[c, pl.ds(t, 1), :], (32, 128))
                g = y if g is None else g + y
            s = jnp.broadcast_to(ss[pl.ds(t, 1), :], (8, 128))
            tot = None
            for j in range(4):
                y = jnp.where(i8 + 8.0 * j == s, g[8 * j:8 * j + 8], 0.0)
                tot = y if tot is None else tot + y
            rows.append(jnp.sum(tot, axis=0, keepdims=True))
        out[pl.ds(b * U, U), :] = jnp.concatenate(rows, 0)
        return 0

    lax.fori_loop(0, LOOPS, body, 0)


def fwd_att(tab, ac, ma, w_tab, out):
    def body(b, _):
        h = jnp.concatenate([onehot(ma, b * U + u, 256) for u in range(U)], 1)
        x = jnp.dot(tab[...], h, preferred_element_type=F32)
        rows = []
        for u in range(U):
            t = b * U + u
            sl = slice(128 * u, 128 * u + 128)
            g = None
            for q in range(4):
                y = (x[SE * q:SE * q + SE, sl] + x[4 * SE + SE * q:4 * SE + SE * q + SE, sl]) * jnp.broadcast_to(ac[q, pl.ds(t, 1), :], (SE, 128))
                g = y if g is None else g + y
            g = g * w_tab[t]
            tot = None
            for j in range(SE // 8):
                y = g[8 * j:8 * j + 8]
                tot = y if tot is None else tot + y
            rows.append(jnp.sum(tot, axis=0, keepdims=True))
        out[pl.ds(b * U, U), :] = jnp.concatenate(rows, 0)
        return 0

    lax.fori_loop(0, LOOPS, body, 0)


def drain(ref, sem):
    pltpu.make_async_copy(ref, ref, sem).wait()


def to_peers(count, me, start):
    def body(i, _):
        start(lax.rem(me + i, count), i)
        return 0

    lax.fori_loop(1, count, body, 0)


def remote(src, dst, send, recv, si, gi):
    pltpu.make_async_remote_copy(src_ref=src, dst_ref=dst, send_sem=send, recv_sem=recv,
                                 device_id=(si, gi), device_id_type=MESH).start()


def kernel(star_h, knot_h, frac_h, sc_h, ac_h, cc_h, obs_h, caln_h, live,
           xs_o, xa_o, xc_o, r_o,
           star, knot, frac, sc, ac, cc, obs, caln, in_sem,
           ms, ss, ma, sa, wk, w_tab, hc, psh, psl, pat, accs, acca,
           gac, gs, rac, rs, fac, fs, halo_v, halo_r, halo_t, halo_n, near,
           dac, dst, tac, tst, img_a, img_s, img, res,
           s1v, s1r, s2v, s2r,
           send_sem, ar_sem, sc_sem):
    me = lax.axis_index("stars")
    seg = lax.axis_index("seg")
    up = lax.rem(seg + 1, NG)
    down = lax.rem(seg + NG - 1, NG)

    loads = [pltpu.make_async_copy(a, b, in_sem.at[k]) for k, (a, b) in enumerate(
        ((star_h, star), (knot_h, knot), (frac_h, frac), (obs_h, obs), (caln_h, caln), (ac_h, ac), (cc_h, cc), (sc_h, sc)))]
    for c in loads:
        c.start()

    barrier = pltpu.get_barrier_semaphore()

    def hello_stars(p, i):
        pl.semaphore_signal(barrier, inc=1, device_id=(p, seg), device_id_type=MESH)

    def hello_seg(p, i):
        pl.semaphore_signal(barrier, inc=1, device_id=(me, p), device_id_type=MESH)

    to_peers(NS, me, hello_stars)
    to_peers(NG, seg, hello_seg)

    for c in loads[:3]:
        c.wait()
    prepare(star, knot, frac, ms, ss, ma, sa, wk, w_tab)
    for c in loads[3:]:
        c.wait()

    mask = jnp.where(iota((128, 128), 0) < live[0], 1.0, 0.0)
    res[...] = obs[...] * mask
    hc[...] = jnp.where(iota((256, 128), 0) == jnp.broadcast_to(caln[...], (256, 128)), 1.0, 0.0).astype(BF)

    lane = iota((8, 128), 1)
    sub = iota((8, 128), 0)

    def backward(n, val_ref):
        v = val_ref[...]
        for q in range(4):
            pat[q] = ac[q] * v
        acca[...] = jnp.zeros_like(acca)
        back_att(0, LOOPS, pat, ma, w_tab, acca)
        hi, lo = split(cc[...] * v)
        cal = jnp.dot(hc[...], hi, preferred_element_type=F32) + jnp.dot(hc[...], lo, preferred_element_type=F32)
        gac[n, 128:256, 0:128] = cal[0:128]
        gac[n, 128:256, 128:256] = cal[128:256]
        row = jnp.zeros((8, 128), F32)
        last = iota((8, 256), 1) == 255
        for q in range(4):
            x = acca[SE * q:SE * q + SE] + acca[4 * SE + SE * q:4 * SE + SE * q + SE]
            spill = x[32:40]
            over = jnp.sum(jnp.where(last, spill, 0.0), axis=1, keepdims=True)
            row = row + jnp.where(lane == 4 * sub + q, jnp.broadcast_to(over, (8, 128)), 0.0)
            moved = jnp.where(iota((8, 256), 1) == 0, 0.0, pltpu.roll(spill, 1, 1))
            gac[n, pl.ds(32 * q, 8), :] = x[0:8] + moved
            gac[n, pl.ds(32 * q + 8, 24), :] = x[8:32]
        halo_v[n] = jnp.sum(row, axis=0, keepdims=True)
        halo_r[n, me] = halo_v[n]
        if n == 0:
            pl.semaphore_wait(barrier, NS - 1 + NG - 1)

        def send_halo(p, i):
            remote(halo_v.at[n], halo_r.at[n, me], send_sem.at[n, 0], ar_sem.at[n, 0], p, seg)

        def send_rs(p, i):
            remote(gac.at[n, pl.ds(pl.multiple_of(8 * p, 8), 8)], rac.at[n, pl.ds(pl.multiple_of(8 * (i - 1), 8), 8)], send_sem.at[n, 1], ar_sem.at[n, 1], p, seg)

        to_peers(NS, me, send_rs)
        to_peers(NS, me, send_halo)

        for c in range(5):
            p = sc[c] * v
            h = p.astype(BF).astype(F32)
            psh[c] = h
            psl[c] = p - h
        accs[...] = jnp.zeros_like(accs)
        back_star(0, LOOPS, psh, psl, ms, ss, accs)
        gs[n] = accs[0:160] + accs[160:320]

        def send_rs_star(p, i):
            remote(gs.at[n, pl.ds(pl.multiple_of(40 * p, 8), 40)], rs.at[n, pl.ds(pl.multiple_of(40 * (i - 1), 8), 40)], send_sem.at[n, 2], ar_sem.at[n, 2], me, p)

        to_peers(NG, seg, send_rs_star)

    def reduce(n):
        drain(halo_r.at[n, pl.ds(0, NS - 1)], ar_sem.at[n, 0])
        t = halo_r[n, 0]
        for i in range(1, NS):
            t = t + halo_r[n, i]
        halo_t[n] = t
        remote(halo_t.at[n], halo_n.at[n], send_sem.at[n, 3], ar_sem.at[n, 3], me, up)

        drain(rac.at[n], ar_sem.at[n, 1])
        own = pl.ds(pl.multiple_of(8 * me, 8), 8)
        t = gac[n, own, :]
        for i in range(NS - 1):
            t = t + rac[n, 8 * i:8 * i + 8, :]
        fac[n, own, :] = t

        def send_ag(p, i):
            remote(fac.at[n, pl.ds(pl.multiple_of(8 * me, 8), 8)], fac.at[n, pl.ds(pl.multiple_of(8 * me, 8), 8)], send_sem.at[n, 4], ar_sem.at[n, 4], p, seg)

        to_peers(NS, me, send_ag)

        drain(rs.at[n], ar_sem.at[n, 2])
        own_s = pl.ds(pl.multiple_of(40 * seg, 8), 40)
        fs[n, own_s, :] = gs[n, own_s, :] + rs[n, 0:40, :] + rs[n, 40:80, :] + rs[n, 80:120, :]

        def send_ag_star(p, i):
            remote(fs.at[n, pl.ds(pl.multiple_of(40 * seg, 8), 40)], fs.at[n, pl.ds(pl.multiple_of(40 * seg, 8), 40)], send_sem.at[n, 5], ar_sem.at[n, 5], me, p)

        to_peers(NG, seg, send_ag_star)

    def gather_att(n, combine):
        drain(halo_n.at[n], ar_sem.at[n, 3])
        drain(fac.at[n, pl.ds(0, 248)], ar_sem.at[n, 4])
        row = jnp.broadcast_to(jnp.where(seg > 0, halo_n[n], 0.0), (8, 128))
        for q in range(4):
            z = jnp.sum(jnp.where(lane == 4 * sub + q, row, 0.0), axis=1, keepdims=True)
            a = pl.ds(32 * q, 8)
            b = pl.ds(32 * q + 8, 24)
            first = jnp.where(iota((8, 256), 1) == 0, jnp.broadcast_to(z, (8, 256)), 0.0)
            dac[n, a, :] = combine(fac[n, a, :] + first, a)
            dac[n, b, :] = combine(fac[n, b, :], b)
        c = pl.ds(128, 128)
        dac[n, c, :] = combine(fac[n, c, :], c)
        for q in range(4):
            remote(dac.at[n, pl.ds(32 * q, 8), pl.ds(0, 128)], near.at[n, pl.ds(8 * q, 8)], send_sem.at[n, 6], ar_sem.at[n, 6], me, down)
        drain(near.at[n], ar_sem.at[n, 6])
        parts = []
        for q in range(4):
            parts.append(dac[n, pl.ds(32 * q, 32), :])
            nb = jnp.where(seg < NG - 1, near[n, pl.ds(8 * q, 8), :], 0.0)
            nb = jnp.broadcast_to(nb[:, 0:1], (8, 256))
            parts.append(jnp.where(iota((8, 256), 1) == 255, nb, pltpu.roll(dac[n, pl.ds(32 * q, 8), :], 255, 1)))
        h, l = split(jnp.concatenate(parts, axis=0))
        tac[0:4 * SE] = h
        tac[4 * SE:8 * SE] = l

    def gather_star(n, combine):
        drain(fs.at[n, pl.ds(0, 120)], ar_sem.at[n, 5])
        c = pl.ds(0, 160)
        dst[n] = combine(fs[n], c)
        h, l = split(dst[n])
        tst[0:160] = h
        tst[160:320] = l

    def put_scalar(k, v):
        s1v[k] = v
        s1r[k, me] = v

        def send(p, i):
            remote(s1v.at[k], s1r.at[k, me], sc_sem.at[k, 0], sc_sem.at[k, 1], p, seg)

        to_peers(NS, me, send)

    def mid_scalar(k):
        drain(s1r.at[k, pl.ds(0, NS - 1)], sc_sem.at[k, 1])
        t = s1r[k, 0]
        for i in range(1, NS):
            t = t + s1r[k, i]
        s2v[k] = t
        s2r[k, seg] = t

        def send(p, i):
            remote(s2v.at[k], s2r.at[k, seg], sc_sem.at[k, 2], sc_sem.at[k, 3], me, p)

        to_peers(NG, seg, send)

    def get_scalar(k):
        drain(s2r.at[k, pl.ds(0, NG - 1)], sc_sem.at[k, 3])
        t = (s2r[k, 0] + s2r[k, 1]) + (s2r[k, 2] + s2r[k, 3])
        return jnp.sum(t, axis=1, keepdims=True)

    def lanes(x):
        t = jnp.sum(x, axis=0, keepdims=True)
        while t.shape[1] > 128:
            h = t.shape[1] // 2
            t = t[:, :h] + t[:, h:]
        return t

    def norm(n):
        a = dac[n]
        s = dst[n]
        return lanes(a * a) * (1.0 / NS) + lanes(s * s) * (1.0 / NG)

    def cal_image(n):
        x = dac[n, pl.ds(128, 128), :]
        x = jnp.concatenate([x[:, 0:128], x[:, 128:256]], axis=0)
        h, l = split(x)
        tn = (((0,), (0,)), ((), ()))
        v = lax.dot_general(hc[...], h, tn, preferred_element_type=F32) + lax.dot_general(hc[...], l, tn, preferred_element_type=F32)
        return cc[...] * v

    def image(n):
        return (img_a[...] + img_s[...] + cal_image(n)) * jnp.where(iota((128, 128), 0) < live[0], 1.0, 0.0)

    def first(x, sl):
        return x

    backward(0, res)
    reduce(0)
    gather_att(0, first)
    gather_star(0, first)
    put_scalar(0, norm(0))
    fwd_att(tac, ac, ma, w_tab, img_a)
    mid_scalar(0)
    fwd_star(tst, sc, ms, ss, img_s)
    img[...] = image(0)
    put_scalar(1, lanes(img[...] * img[...]))

    backward(1, img)
    mid_scalar(1)
    reduce(1)
    gg0 = get_scalar(0)
    alpha0 = gg0 / get_scalar(1)
    gather_att(1, lambda x, sl: dac[0, sl, :] - alpha0 * x)
    gather_star(1, lambda x, sl: dst[0, sl, :] - alpha0 * x)
    put_scalar(2, norm(1))
    fwd_att(tac, ac, ma, w_tab, img_a)
    mid_scalar(2)
    fwd_star(tst, sc, ms, ss, img_s)
    gg1 = get_scalar(2)
    beta = gg1 / gg0
    img1 = image(1) + beta * img[...]
    put_scalar(3, lanes(img1 * img1))
    res[...] = res[...] - alpha0 * img[...]
    img[...] = img1
    mid_scalar(3)
    alpha1 = gg1 / get_scalar(3)
    ab = alpha0 + alpha1 * beta
    r_o[...] = res[...] - alpha1 * img[...]
    xs_o[...] = ab * dst[0] + alpha1 * dst[1]
    x = ab * dac[0] + alpha1 * dac[1]
    xa_o[...] = x[0:128]
    xc_o[0:128] = x[128:256, 0:128]
    xc_o[128:256] = x[128:256, 128:256]

    for n in range(2):
        drain(halo_r.at[n, pl.ds(0, NS - 1)], send_sem.at[n, 0])
        drain(rac.at[n], send_sem.at[n, 1])
        drain(rs.at[n], send_sem.at[n, 2])
        drain(halo_n.at[n], send_sem.at[n, 3])
        drain(fac.at[n, pl.ds(0, 248)], send_sem.at[n, 4])
        drain(fs.at[n, pl.ds(0, 120)], send_sem.at[n, 5])
        drain(near.at[n], send_sem.at[n, 6])
    for k in range(4):
        drain(s1r.at[k, pl.ds(0, NS - 1)], sc_sem.at[k, 0])
        drain(s2r.at[k, pl.ds(0, NG - 1)], sc_sem.at[k, 2])


def on_device(star, knot, frac, sc, ac, cc, tile_cal, live, obs):
    shape = jax.ShapeDtypeStruct
    T = (128, 128)
    hbm = pl.BlockSpec(memory_space=pl.ANY)
    vm = pl.BlockSpec(memory_space=pltpu.VMEM)
    V = pltpu.VMEM
    sem = pltpu.SemaphoreType.DMA
    xs, xa, xc, r = pl.pallas_call(
        kernel,
        in_specs=[hbm] * 8 + [pl.BlockSpec(memory_space=pltpu.SMEM)],
        out_specs=[vm] * 4,
        out_shape=[shape((160, 256), F32), shape((128, 256), F32), shape((256, 128), F32), shape(T, F32)],
        scratch_shapes=[
            V(T, jnp.int32), V(T, jnp.int32), V(T, F32), V((5,) + T, F32), V((4,) + T, F32), V(T, F32), V(T, F32),
            V((1, 128), jnp.int32), sem((8,)),
            V(T, F32), V(T, F32), V(T, F32), V(T, jnp.int32), V((4,) + T, F32), V((128, SE, 128), F32),
            V((256, 128), BF), V((5,) + T, F32), V((5,) + T, F32), V((4,) + T, F32), V((320, 256), F32), V((320, 256), F32),
            V((2, 256, 256), F32), V((2, 160, 256), F32), V((2, 248, 256), F32), V((2, 120, 256), F32),
            V((2, 256, 256), F32), V((2, 160, 256), F32),
            V((2, 1, 128), F32), V((2, NS, 1, 128), F32), V((2, 1, 128), F32), V((2, 1, 128), F32), V((2, 32, 128), F32),
            V((2, 256, 256), F32), V((2, 160, 256), F32), V((320, 256), BF), V((320, 256), BF),
            V(T, F32), V(T, F32), V(T, F32), V(T, F32),
            V((4, 1, 128), F32), V((4, NS, 1, 128), F32), V((4, 1, 128), F32), V((4, NG, 1, 128), F32),
            sem((2, 7)), sem((2, 7)), sem((4, 4)),
        ],
        compiler_params=pltpu.CompilerParams(collective_id=0, has_side_effects=True, vmem_limit_bytes=60 << 20),
        name="solve",
    )(star, knot, frac, sc, ac, cc, obs, tile_cal.reshape(1, 128), live)
    return xs.reshape(5, 8192), jnp.swapaxes(xa.reshape(4, 32, 256), 1, 2).reshape(4, 8192), xc, r


def solution(mesh):
    P = jax.sharding.PartitionSpec
    a = P(("stars", "seg"), None)
    b = P(None, ("stars", "seg"), None)
    c = P(("stars", "seg"))
    return jax.shard_map(on_device, mesh=mesh, in_specs=(a, a, a, b, b, a, c, c, a),
                         out_specs=(P(None, "stars"), P(None, "seg"), P("seg", None), a), check_vma=False)
```

```python
import jax
import jax.numpy as jnp
from jax import lax
from jax.experimental import pallas as pl
from jax.experimental.pallas import tpu as pltpu

BF = jnp.bfloat16
F32 = jnp.float32
SE = 40
U = 32
LOOPS = 128 // U
NS = 32
NG = 4
MESH = pl.DeviceIdType.MESH


def split(x):
    hi = x.astype(BF)
    return hi, (x - hi.astype(F32)).astype(BF)


def row16(ref, t):
    return jnp.broadcast_to(ref[pl.ds(t, 1), :], (16, 128)).astype(BF)


def iota16():
    return lax.broadcasted_iota(jnp.int32, (16, 128), 0).astype(F32).astype(BF)


def onehot(ref, t, n):
    r = row16(ref, t)
    i = iota16()
    one = jnp.ones((16, 128), BF)
    zero = jnp.zeros((16, 128), BF)
    return jnp.concatenate([jnp.where(i + BF(16 * k) == r, one, zero) for k in range(n // 16)], axis=0)


def iota(shape, axis):
    return lax.broadcasted_iota(jnp.int32, shape, axis)


def prepare(star, knot, frac, ms, ss, ma, sa, wk, w_tab):
    s = star[...]
    k = knot[...]
    ms[...] = (s & 255).astype(F32)
    ss[...] = (s >> 8).astype(F32)
    ma[...] = (k >> 5).astype(F32)
    sa[...] = k & 31
    u = frac[...]
    rem = 1.0 - u
    sq = u * u
    cu = sq * u
    wk[0] = rem * rem * rem / 6.0
    wk[1] = (3.0 * cu - 6.0 * sq + 4.0) / 6.0
    wk[2] = (-3.0 * cu + 3.0 * sq + 3.0 * u + 1.0) / 6.0
    wk[3] = cu / 6.0

    def body(t, _):
        kk = jnp.broadcast_to(sa[pl.ds(t, 1), :], (8, 128))
        w = [jnp.broadcast_to(wk[j, pl.ds(t, 1), :], (8, 128)) for j in range(4)]
        base = iota((8, 128), 0) - kk
        for j in range(SE // 8):
            d = base + 8 * j
            v = jnp.where(d == 0, w[0], jnp.where(d == 1, w[1], jnp.where(d == 2, w[2], jnp.where(d == 3, w[3], 0.0))))
            w_tab[t, pl.ds(8 * j, 8), :] = v
        return 0

    lax.fori_loop(0, 128, body, 0)


DN = (((1,), (1,)), ((), ()))


def back_att(start, stop, pat, ma, w_tab, acc):
    def body(b, _):
        hs = []
        rows = []
        for u in range(U):
            t = b * U + u
            hs.append(onehot(ma, t, 256))
            w = w_tab[t]
            a = jnp.concatenate([w * jnp.broadcast_to(pat[q, pl.ds(t, 1), :], (SE, 128)) for q in range(4)], axis=0)
            h, l = split(a)
            rows.append(jnp.concatenate([h, l], axis=0))
        acc[...] += lax.dot_general(jnp.concatenate(rows, 1), jnp.concatenate(hs, 1), DN, preferred_element_type=F32)
        return 0

    lax.fori_loop(start, stop, body, 0)


def back_star(start, stop, psh, psl, ms, ss, acc):
    z16 = jnp.zeros((16, 128), BF)

    def body(b, _):
        hs = []
        rows = []
        for u in range(U):
            t = b * U + u
            hs.append(onehot(ms, t, 256))
            r = row16(ss, t)
            i = iota16()
            masks = [(i + BF(16 * k)) == r for k in range(2)]
            his = []
            los = []
            for c in range(5):
                h = row16(psh.at[c], t)
                l = row16(psl.at[c], t)
                his += [jnp.where(m, h, z16) for m in masks]
                los += [jnp.where(m, l, z16) for m in masks]
            rows.append(jnp.concatenate(his + los, axis=0))
        acc[...] += lax.dot_general(jnp.concatenate(rows, 1), jnp.concatenate(hs, 1), DN, preferred_element_type=F32)
        return 0

    lax.fori_loop(start, stop, body, 0)


def fwd_star(tab, sc, ms, ss, out):
    i8 = iota((8, 128), 0).astype(F32)

    def body(b, _):
        h = jnp.concatenate([onehot(ms, b * U + u, 256) for u in range(U)], 1)
        x = jnp.dot(tab[...], h, preferred_element_type=F32)
        rows = []
        for u in range(U):
            t = b * U + u
            sl = slice(128 * u, 128 * u + 128)
            g = None
            for c in range(5):
                y = (x[32 * c:32 * c + 32, sl] + x[160 + 32 * c:192 + 32 * c, sl]) * jnp.broadcast_to(sc[c, pl.ds(t, 1), :], (32, 128))
                g = y if g is None else g + y
            s = jnp.broadcast_to(ss[pl.ds(t, 1), :], (8, 128))
            tot = None
            for j in range(4):
                y = jnp.where(i8 + 8.0 * j == s, g[8 * j:8 * j + 8], 0.0)
                tot = y if tot is None else tot + y
            rows.append(jnp.sum(tot, axis=0, keepdims=True))
        out[pl.ds(b * U, U), :] = jnp.concatenate(rows, 0)
        return 0

    lax.fori_loop(0, LOOPS, body, 0)


def fwd_att(tab, ac, ma, w_tab, out):
    def body(b, _):
        h = jnp.concatenate([onehot(ma, b * U + u, 256) for u in range(U)], 1)
        x = jnp.dot(tab[...], h, preferred_element_type=F32)
        rows = []
        for u in range(U):
            t = b * U + u
            sl = slice(128 * u, 128 * u + 128)
            g = None
            for q in range(4):
                y = (x[SE * q:SE * q + SE, sl] + x[4 * SE + SE * q:4 * SE + SE * q + SE, sl]) * jnp.broadcast_to(ac[q, pl.ds(t, 1), :], (SE, 128))
                g = y if g is None else g + y
            g = g * w_tab[t]
            tot = None
            for j in range(SE // 8):
                y = g[8 * j:8 * j + 8]
                tot = y if tot is None else tot + y
            rows.append(jnp.sum(tot, axis=0, keepdims=True))
        out[pl.ds(b * U, U), :] = jnp.concatenate(rows, 0)
        return 0

    lax.fori_loop(0, LOOPS, body, 0)


def drain(ref, sem):
    pltpu.make_async_copy(ref, ref, sem).wait()


def to_peers(count, me, start):
    def body(i, _):
        start(lax.rem(me + i, count), i)
        return 0

    lax.fori_loop(1, count, body, 0)


def remote(src, dst, send, recv, si, gi):
    pltpu.make_async_remote_copy(src_ref=src, dst_ref=dst, send_sem=send, recv_sem=recv,
                                 device_id=(si, gi), device_id_type=MESH).start()


def kernel(star_h, knot_h, frac_h, sc_h, ac_h, cc_h, obs_h, caln_h, live,
           xs_h, xa_h, xc_h, r_h,
           star, knot, frac, sc, ac, cc, obs, caln, in_sem,
           ms, ss, ma, sa, wk, w_tab, hc, psh, psl, pat, accs, acca,
           gac, gs, rac, rs, fac, fs, halo_v, halo_r, halo_t, halo_d, halo_u, ahead,
           dac, dst, tac, tst, img_a, img_s, img, res,
           s1v, s1r, s2v, s2r,
           send_sem, ar_sem, sc_sem):
    me = lax.axis_index("stars")
    seg = lax.axis_index("seg")
    up = lax.rem(seg + 1, NG)
    down = lax.rem(seg + NG - 1, NG)

    loads = [pltpu.make_async_copy(a, b, in_sem.at[k]) for k, (a, b) in enumerate(
        ((star_h, star), (knot_h, knot), (frac_h, frac), (obs_h, obs), (caln_h, caln), (ac_h, ac), (cc_h, cc), (sc_h, sc)))]
    for c in loads:
        c.start()

    barrier = pltpu.get_barrier_semaphore()

    def hello_stars(p, i):
        pl.semaphore_signal(barrier, inc=1, device_id=(p, seg), device_id_type=MESH)

    def hello_seg(p, i):
        pl.semaphore_signal(barrier, inc=1, device_id=(me, p), device_id_type=MESH)

    to_peers(NS, me, hello_stars)
    to_peers(NG, seg, hello_seg)

    for c in loads[:3]:
        c.wait()
    prepare(star, knot, frac, ms, ss, ma, sa, wk, w_tab)
    for c in loads[3:]:
        c.wait()

    mask = jnp.where(iota((128, 128), 0) < live[0], 1.0, 0.0)
    res[...] = obs[...] * mask
    hc[...] = jnp.where(iota((256, 128), 0) == jnp.broadcast_to(caln[...], (256, 128)), 1.0, 0.0).astype(BF)

    lane = iota((8, 128), 1)
    sub = iota((8, 128), 0)
    own = pl.ds(pl.multiple_of(8 * me, 8), 8)
    own_s = pl.ds(pl.multiple_of(40 * seg, 8), 40)

    def column(row, q):
        return jnp.sum(jnp.where((lane == 4 * sub + q) & (sub < 3), jnp.broadcast_to(row, (8, 128)), 0.0), axis=1, keepdims=True)

    def backward(n, val_ref, between):
        v = val_ref[...]
        for q in range(4):
            pat[q] = ac[q] * v
        acca[...] = jnp.zeros_like(acca)
        back_att(0, LOOPS, pat, ma, w_tab, acca)
        hi, lo = split(cc[...] * v)
        cal = jnp.dot(hc[...], hi, preferred_element_type=F32) + jnp.dot(hc[...], lo, preferred_element_type=F32)
        gac[n, 128:256, 0:128] = cal[0:128]
        gac[n, 128:256, 128:256] = cal[128:256]
        row = jnp.zeros((8, 128), F32)
        wide = iota((8, 256), 1)
        for q in range(4):
            x = acca[SE * q:SE * q + SE] + acca[4 * SE + SE * q:4 * SE + SE * q + SE]
            spill = x[32:40]
            over = jnp.sum(jnp.where(wide == 255, spill, 0.0), axis=1, keepdims=True)
            row = row + jnp.where((lane == 4 * sub + q) & (sub < 3), jnp.broadcast_to(over, (8, 128)), 0.0)
            row = row + jnp.where((lane == 16 + 4 * sub + q) & (sub < 3), jnp.broadcast_to(x[0:8, 0:1], (8, 128)), 0.0)
            moved = jnp.where(wide == 0, 0.0, pltpu.roll(spill, 1, 1))
            gac[n, pl.ds(32 * q, 8), :] = x[0:8] + moved
            gac[n, pl.ds(32 * q + 8, 24), :] = x[8:32]
        halo_v[n] = jnp.sum(row, axis=0, keepdims=True)
        halo_r[n, me] = halo_v[n]
        if n == 0:
            pl.semaphore_wait(barrier, NS - 1 + NG - 1)

        def send_halo(p, i):
            remote(halo_v.at[n], halo_r.at[n, me], send_sem.at[n, 0], ar_sem.at[n, 0], p, seg)

        def send_rs(p, i):
            remote(gac.at[n, pl.ds(pl.multiple_of(8 * p, 8), 8)], rac.at[n, pl.ds(pl.multiple_of(8 * (i - 1), 8), 8)],
                   send_sem.at[n, 1], ar_sem.at[n, 1], p, seg)

        to_peers(NS, me, send_rs)
        to_peers(NS, me, send_halo)
        between()

        for c in range(5):
            p = sc[c] * v
            h = p.astype(BF).astype(F32)
            psh[c] = h
            psl[c] = p - h
        accs[...] = jnp.zeros_like(accs)
        back_star(0, LOOPS, psh, psl, ms, ss, accs)
        gs[n] = accs[0:160] + accs[160:320]

        def send_rs_star(p, i):
            remote(gs.at[n, pl.ds(pl.multiple_of(40 * p, 8), 40)], rs.at[n, pl.ds(pl.multiple_of(40 * (i - 1), 8), 40)],
                   send_sem.at[n, 2], ar_sem.at[n, 2], me, p)

        to_peers(NG, seg, send_rs_star)

    def reduce_att(n):
        drain(rac.at[n], ar_sem.at[n, 1])
        t = gac[n, own, :]
        for i in range(NS - 1):
            t = t + rac[n, 8 * i:8 * i + 8, :]
        fac[n, own, :] = t

        def send_ag(p, i):
            remote(fac.at[n, own], fac.at[n, own], send_sem.at[n, 4], ar_sem.at[n, 4], p, seg)

        to_peers(NS, me, send_ag)

        drain(halo_r.at[n, pl.ds(0, NS - 1)], ar_sem.at[n, 0])
        t = halo_r[n, 0]
        for i in range(1, NS):
            t = t + halo_r[n, i]
        halo_t[n] = t
        remote(halo_t.at[n], halo_d.at[n], send_sem.at[n, 3], ar_sem.at[n, 3], me, up)
        remote(halo_t.at[n], halo_u.at[n], send_sem.at[n, 6], ar_sem.at[n, 6], me, down)

    def reduce_star(n):
        drain(rs.at[n], ar_sem.at[n, 2])
        fs[n, own_s, :] = gs[n, own_s, :] + rs[n, 0:40, :] + rs[n, 40:80, :] + rs[n, 80:120, :]

        def send_ag_star(p, i):
            remote(fs.at[n, own_s], fs.at[n, own_s], send_sem.at[n, 5], ar_sem.at[n, 5], me, p)

        to_peers(NG, seg, send_ag_star)

    def from_below(n):
        return jnp.where(seg > 0, halo_d[n], 0.0)

    def first_knots(n, q):
        return jnp.where(iota((8, 256), 1) == 0, jnp.broadcast_to(column(from_below(n), q), (8, 256)), 0.0)

    def halo(n, combine):
        drain(halo_d.at[n], ar_sem.at[n, 3])
        drain(halo_u.at[n], ar_sem.at[n, 6])
        t = pltpu.roll(jnp.broadcast_to(halo_u[n], (8, 128)), 112, 1)[0:1] + halo_t[n]
        ahead[n] = combine(jnp.where(seg < NG - 1, t, 0.0), ahead, slice(None))

    def own_norm(n, combine):
        mine = jnp.where((lax.rem(me, 4) == 0) & (me < 16), 1.0, 0.0)
        a = combine(fac[n, own, :] + mine * first_knots(n, me // 4), dac, own)
        s = combine(fs[n, own_s, :], dst, own_s)
        return lanes(a * a) + lanes(s * s)

    def gather_att(n, combine):
        drain(fac.at[n, pl.ds(0, 248)], ar_sem.at[n, 4])
        parts = []
        for q in range(4):
            a = pl.ds(32 * q, 8)
            b = pl.ds(32 * q + 8, 24)
            x = combine(fac[n, a, :] + first_knots(n, q), dac, a)
            y = combine(fac[n, b, :], dac, b)
            dac[n, a, :] = x
            dac[n, b, :] = y
            nb = jnp.broadcast_to(column(ahead[n], q), (8, 256))
            parts += [x, y, jnp.where(iota((8, 256), 1) == 255, nb, pltpu.roll(x, 255, 1))]
        c = pl.ds(128, 128)
        dac[n, c, :] = combine(fac[n, c, :], dac, c)
        h, l = split(jnp.concatenate(parts, axis=0))
        tac[0:4 * SE] = h
        tac[4 * SE:8 * SE] = l

    def gather_star(n, combine):
        drain(fs.at[n, pl.ds(0, 120)], ar_sem.at[n, 5])
        x = combine(fs[n], dst, slice(None))
        dst[n] = x
        h, l = split(x)
        tst[0:160] = h
        tst[160:320] = l

    def put_scalar(k, v):
        s1v[k] = v
        s1r[k, me] = v

        def send(p, i):
            remote(s1v.at[k], s1r.at[k, me], sc_sem.at[k, 0], sc_sem.at[k, 1], p, seg)

        to_peers(NS, me, send)

    def mid_scalar(k):
        drain(s1r.at[k, pl.ds(0, NS - 1)], sc_sem.at[k, 1])
        t = s1r[k, 0]
        for i in range(1, NS):
            t = t + s1r[k, i]
        s2v[k] = t
        s2r[k, seg] = t

        def send(p, i):
            remote(s2v.at[k], s2r.at[k, seg], sc_sem.at[k, 2], sc_sem.at[k, 3], me, p)

        to_peers(NG, seg, send)

    def get_scalar(k):
        drain(s2r.at[k, pl.ds(0, NG - 1)], sc_sem.at[k, 3])
        t = (s2r[k, 0] + s2r[k, 1]) + (s2r[k, 2] + s2r[k, 3])
        return jnp.sum(t, axis=1, keepdims=True)

    def lanes(x):
        t = jnp.sum(x, axis=0, keepdims=True)
        while t.shape[1] > 128:
            h = t.shape[1] // 2
            t = t[:, :h] + t[:, h:]
        return t

    def cal_image(n):
        x = dac[n, pl.ds(128, 128), :]
        x = jnp.concatenate([x[:, 0:128], x[:, 128:256]], axis=0)
        h, l = split(x)
        tn = (((0,), (0,)), ((), ()))
        v = lax.dot_general(hc[...], h, tn, preferred_element_type=F32) + lax.dot_general(hc[...], l, tn, preferred_element_type=F32)
        return cc[...] * v

    def reduce(n, combine):
        reduce_att(n)
        reduce_star(n)
        halo(n, combine)
        put_scalar(2 * n, own_norm(n, combine))

    def forward(n, combine):
        gather_att(n, combine)
        fwd_att(tac, ac, ma, w_tab, img_a)
        extra = cal_image(n)
        gather_star(n, combine)
        img_a[...] += extra
        mid_scalar(2 * n)
        fwd_star(tst, sc, ms, ss, img_s)
        return (img_a[...] + img_s[...]) * jnp.where(iota((128, 128), 0) < live[0], 1.0, 0.0)

    def plain(x, ref, sl):
        return x

    backward(0, res, lambda: None)
    reduce(0, plain)
    img[...] = forward(0, plain)
    put_scalar(1, lanes(img[...] * img[...]))
    backward(1, img, lambda: mid_scalar(1))
    gg0 = get_scalar(0)
    alpha0 = gg0 / get_scalar(1)

    def step(x, ref, sl):
        return ref[0, sl] - alpha0 * x

    reduce(1, step)
    img1 = forward(1, step)
    gg1 = get_scalar(2)
    beta = gg1 / gg0
    img1 = img1 + beta * img[...]
    put_scalar(3, lanes(img1 * img1))
    res[...] = res[...] - alpha0 * img[...]
    img[...] = img1
    for n in range(2):
        drain(halo_r.at[n, pl.ds(0, NS - 1)], send_sem.at[n, 0])
        drain(rac.at[n], send_sem.at[n, 1])
        drain(rs.at[n], send_sem.at[n, 2])
        drain(halo_d.at[n], send_sem.at[n, 3])
        drain(fac.at[n, pl.ds(0, 248)], send_sem.at[n, 4])
        drain(fs.at[n, pl.ds(0, 120)], send_sem.at[n, 5])
        drain(halo_u.at[n], send_sem.at[n, 6])
    mid_scalar(3)
    alpha1 = gg1 / get_scalar(3)
    ab = alpha0 + alpha1 * beta
    res[...] = res[...] - alpha1 * img[...]
    fs[0] = ab * dst[0] + alpha1 * dst[1]
    fac[0] = ab * dac[0] + alpha1 * dac[1]
    stores = [pltpu.make_async_copy(a, b, in_sem.at[k]) for k, (a, b) in enumerate(
        ((fs.at[0], xs_h), (fac.at[0, pl.ds(0, 128)], xa_h), (fac.at[0, pl.ds(128, 128)], xc_h), (res, r_h)))]
    for c in stores:
        c.start()

    for k in range(4):
        drain(s1r.at[k, pl.ds(0, NS - 1)], sc_sem.at[k, 0])
        drain(s2r.at[k, pl.ds(0, NG - 1)], sc_sem.at[k, 2])
    for c in stores:
        c.wait()


def finish(xs_h, xa_h, xc_h, r_h, os_h, oa_h, oc_h, or_h, xs, xa, xc, r, os_, oa, oc, sem_in, sem_out):
    loads = [pltpu.make_async_copy(a, b, sem_in.at[k]) for k, (a, b) in enumerate(((xa_h, xa), (xs_h, xs), (xc_h, xc), (r_h, r)))]
    for c in loads:
        c.start()
    loads[0].wait()
    x = xa[...]
    h = x.astype(BF)
    rest = x - h.astype(F32)
    m = rest.astype(BF)
    l = (rest - m.astype(F32)).astype(BF)
    col = iota((256, 256), 1)
    pick = jnp.where(iota((256, 256), 0) == 4 * (col & 63) + (col >> 6), 1.0, 0.0).astype(BF)
    y = jnp.dot(jnp.concatenate([h, m, l], axis=0), pick, preferred_element_type=F32)
    y = (y[0:128] + y[128:256]) + y[256:384]
    for q in range(4):
        z = y[32 * q:32 * q + 32]
        a, b = z[:, 0:128], z[:, 128:256]
        t = jnp.concatenate([a, pltpu.roll(a, 64, 1), b, pltpu.roll(b, 64, 1)], axis=0).T
        for i in range(64):
            oa[q:q + 1, 128 * i:128 * i + 128] = t[i:i + 1]
    for c in loads[1:]:
        c.wait()
    for c in range(5):
        for i in range(32):
            os_[c:c + 1, 256 * i:256 * i + 256] = xs[32 * c + i:32 * c + i + 1]
    oc[0:128] = xc[:, 0:128]
    oc[128:256] = xc[:, 128:256]
    stores = [pltpu.make_async_copy(a, b, sem_out.at[k]) for k, (a, b) in enumerate(((oa, oa_h), (os_, os_h), (oc, oc_h), (r, or_h)))]
    for c in stores:
        c.start()
    for c in stores:
        c.wait()


def on_device(star, knot, frac, sc, ac, cc, tile_cal, live, obs):
    shape = jax.ShapeDtypeStruct
    T = (128, 128)
    hbm = pl.BlockSpec(memory_space=pl.ANY)
    V = pltpu.VMEM
    sem = pltpu.SemaphoreType.DMA
    parts = pl.pallas_call(
        kernel,
        in_specs=[hbm] * 8 + [pl.BlockSpec(memory_space=pltpu.SMEM)],
        out_specs=[hbm] * 4,
        out_shape=[shape((160, 256), F32), shape((128, 256), F32), shape((128, 256), F32), shape(T, F32)],
        scratch_shapes=[
            V(T, jnp.int32), V(T, jnp.int32), V(T, F32), V((5,) + T, F32), V((4,) + T, F32), V(T, F32), V(T, F32),
            V((1, 128), jnp.int32), sem((8,)),
            V(T, F32), V(T, F32), V(T, F32), V(T, jnp.int32), V((4,) + T, F32), V((128, SE, 128), F32),
            V((256, 128), BF), V((5,) + T, F32), V((5,) + T, F32), V((4,) + T, F32), V((320, 256), F32), V((320, 256), F32),
            V((2, 256, 256), F32), V((2, 160, 256), F32), V((2, 248, 256), F32), V((2, 120, 256), F32),
            V((2, 256, 256), F32), V((2, 160, 256), F32),
            V((2, 1, 128), F32), V((2, NS, 1, 128), F32), V((2, 1, 128), F32), V((2, 1, 128), F32), V((2, 1, 128), F32), V((2, 1, 128), F32),
            V((2, 256, 256), F32), V((2, 160, 256), F32), V((320, 256), BF), V((320, 256), BF),
            V(T, F32), V(T, F32), V(T, F32), V(T, F32),
            V((4, 1, 128), F32), V((4, NS, 1, 128), F32), V((4, 1, 128), F32), V((4, NG, 1, 128), F32),
            sem((2, 7)), sem((2, 7)), sem((4, 4)),
        ],
        compiler_params=pltpu.CompilerParams(collective_id=0, has_side_effects=True, vmem_limit_bytes=60 << 20),
        name="solve",
    )(star, knot, frac, sc, ac, cc, obs, tile_cal.reshape(1, 128), live)
    return pl.pallas_call(
        finish,
        in_specs=[hbm] * 4,
        out_specs=[hbm] * 4,
        out_shape=[shape((5, 8192), F32), shape((4, 8192), F32), shape((256, 128), F32), shape(T, F32)],
        scratch_shapes=[V((160, 256), F32), V((128, 256), F32), V((128, 256), F32), V(T, F32),
                        V((5, 8192), F32), V((4, 8192), F32), V((256, 128), F32), sem((4,)), sem((4,))],
        compiler_params=pltpu.CompilerParams(vmem_limit_bytes=60 << 20),
        name="finish",
    )(*parts)


def solution(mesh):
    P = jax.sharding.PartitionSpec
    a = P(("stars", "seg"), None)
    b = P(None, ("stars", "seg"), None)
    c = P(("stars", "seg"))
    return jax.shard_map(on_device, mesh=mesh, in_specs=(a, a, a, b, b, a, c, c, a),
                         out_specs=(P(None, "stars"), P(None, "seg"), P("seg", None), a), check_vma=False)
```

```python
import jax
import jax.numpy as jnp
from jax import lax
from jax.experimental import pallas as pl
from jax.experimental.pallas import tpu as pltpu

BF = jnp.bfloat16
F32 = jnp.float32
SE = 40
U = 32
LOOPS = 128 // U
ROWS = 32
STEP = (128 - ROWS) // LOOPS
NS = 32
NG = 4
MESH = pl.DeviceIdType.MESH


def split(x):
    hi = x.astype(BF)
    return hi, (x - hi.astype(F32)).astype(BF)


def row16(ref, t):
    return jnp.broadcast_to(ref[pl.ds(t, 1), :], (16, 128)).astype(BF)


def iota16():
    return lax.broadcasted_iota(jnp.int32, (16, 128), 0).astype(F32).astype(BF)


def onehot(ref, t, n):
    r = row16(ref, t)
    i = iota16()
    one = jnp.ones((16, 128), BF)
    zero = jnp.zeros((16, 128), BF)
    return jnp.concatenate([jnp.where(i + BF(16 * k) == r, one, zero) for k in range(n // 16)], axis=0)


def iota(shape, axis):
    return lax.broadcasted_iota(jnp.int32, shape, axis)


def prepare(star, knot, frac, ms, ss, ma, sa, lo7, hi6, wk, w_tab):
    s = star[...]
    k = knot[...]
    ms[...] = (s & 255).astype(F32)
    ss[...] = (s >> 8).astype(F32)
    ma[...] = (k >> 5).astype(F32)
    sa[...] = k & 31
    lo7[...] = s[0:ROWS] & 127
    hi6[...] = s[0:ROWS] >> 7
    u = frac[...]
    rem = 1.0 - u
    sq = u * u
    cu = sq * u
    wk[0] = rem * rem * rem / 6.0
    wk[1] = (3.0 * cu - 6.0 * sq + 4.0) / 6.0
    wk[2] = (-3.0 * cu + 3.0 * sq + 3.0 * u + 1.0) / 6.0
    wk[3] = cu / 6.0

    def body(b, _):
        for u in range(8):
            t = b * 8 + u
            kk = jnp.broadcast_to(sa[pl.ds(t, 1), :], (8, 128))
            w = [jnp.broadcast_to(wk[j, pl.ds(t, 1), :], (8, 128)) for j in range(4)]
            base = iota((8, 128), 0) - kk
            for j in range(SE // 8):
                d = base + 8 * j
                v = jnp.where(d == 0, w[0], jnp.where(d == 1, w[1], jnp.where(d == 2, w[2], jnp.where(d == 3, w[3], 0.0))))
                w_tab[t, pl.ds(8 * j, 8), :] = v
        return 0

    lax.fori_loop(0, 16, body, 0)


DN = (((1,), (1,)), ((), ()))


def back_att(start, stop, pat, ma, w_tab, acc):
    def body(b, _):
        hs = []
        rows = []
        for u in range(U):
            t = b * U + u
            hs.append(onehot(ma, t, 256))
            w = w_tab[t]
            a = jnp.concatenate([w * jnp.broadcast_to(pat[q, pl.ds(t, 1), :], (SE, 128)) for q in range(4)], axis=0)
            h, l = split(a)
            rows.append(jnp.concatenate([h, l], axis=0))
        acc[...] += lax.dot_general(jnp.concatenate(rows, 1), jnp.concatenate(hs, 1), DN, preferred_element_type=F32)
        return 0

    lax.fori_loop(start, stop, body, 0)


def back_star(start, stop, psh, psl, ms, ss, acc):
    z16 = jnp.zeros((16, 128), BF)

    def body(b, _):
        hs = []
        rows = []
        for u in range(U):
            t = b * U + u
            hs.append(onehot(ms, t, 256))
            r = row16(ss, t)
            i = iota16()
            masks = [(i + BF(16 * k)) == r for k in range(2)]
            his = []
            los = []
            for c in range(5):
                h = row16(psh.at[c], t)
                l = row16(psl.at[c], t)
                his += [jnp.where(m, h, z16) for m in masks]
                los += [jnp.where(m, l, z16) for m in masks]
            rows.append(jnp.concatenate(his + los, axis=0))
        acc[...] += lax.dot_general(jnp.concatenate(rows, 1), jnp.concatenate(hs, 1), DN, preferred_element_type=F32)
        return 0

    lax.fori_loop(start, stop, body, 0)


def fwd_star(tab, full, sc, ms, ss, lo7, hi6, out):
    i8 = iota((8, 128), 0).astype(F32)

    def body(b, _):
        base = ROWS + b * STEP
        h = jnp.concatenate([onehot(ms, base + u, 256) for u in range(STEP)], 1)
        x = jnp.dot(tab[...], h, preferred_element_type=F32)
        for k in range(ROWS // 8 // LOOPS):
            r0 = pl.ds(pl.multiple_of((b * (ROWS // 8 // LOOPS) + k) * 8, 8), 8)
            lo = lo7[r0, :]
            hi = hi6[r0, :]
            acc = [jnp.zeros((8, 128), F32)] * 5
            for r in range(64):
                m = hi == r
                for c in range(5):
                    t = full[32 * c + r // 2:32 * c + r // 2 + 1, 128 * (r % 2):128 * (r % 2) + 128]
                    t = jnp.take_along_axis(jnp.broadcast_to(t, (8, 128)), lo, axis=1)
                    acc[c] = jnp.where(m, t, acc[c])
            t = acc[0] * sc[0, r0, :]
            for c in range(1, 5):
                t = t + acc[c] * sc[c, r0, :]
            out[r0, :] = t
        rows = []
        for u in range(STEP):
            t = base + u
            sl = slice(128 * u, 128 * u + 128)
            g = None
            for c in range(5):
                y = (x[32 * c:32 * c + 32, sl] + x[160 + 32 * c:192 + 32 * c, sl]) * jnp.broadcast_to(sc[c, pl.ds(t, 1), :], (32, 128))
                g = y if g is None else g + y
            s = jnp.broadcast_to(ss[pl.ds(t, 1), :], (8, 128))
            tot = None
            for j in range(4):
                y = jnp.where(i8 + 8.0 * j == s, g[8 * j:8 * j + 8], 0.0)
                tot = y if tot is None else tot + y
            rows.append(jnp.sum(tot, axis=0, keepdims=True))
        out[pl.ds(pl.multiple_of(base, 8), STEP), :] = jnp.concatenate(rows, 0)
        return 0

    lax.fori_loop(0, LOOPS, body, 0)


def fwd_att(tab, ac, ma, w_tab, out):
    def body(b, _):
        h = jnp.concatenate([onehot(ma, b * U + u, 256) for u in range(U)], 1)
        x = jnp.dot(tab[...], h, preferred_element_type=F32)
        rows = []
        for u in range(U):
            t = b * U + u
            sl = slice(128 * u, 128 * u + 128)
            g = None
            for q in range(4):
                y = (x[SE * q:SE * q + SE, sl] + x[4 * SE + SE * q:4 * SE + SE * q + SE, sl]) * jnp.broadcast_to(ac[q, pl.ds(t, 1), :], (SE, 128))
                g = y if g is None else g + y
            g = g * w_tab[t]
            tot = None
            for j in range(SE // 8):
                y = g[8 * j:8 * j + 8]
                tot = y if tot is None else tot + y
            rows.append(jnp.sum(tot, axis=0, keepdims=True))
        out[pl.ds(b * U, U), :] = jnp.concatenate(rows, 0)
        return 0

    lax.fori_loop(0, LOOPS, body, 0)


def tree(xs):
    while len(xs) > 1:
        xs = [a + b for a, b in zip(xs[::2], xs[1::2])]
    return xs[0]


def drain(ref, sem):
    pltpu.make_async_copy(ref, ref, sem).wait()


def to_peers(count, me, start):
    def body(i, _):
        start(lax.rem(me + i, count), i)
        return 0

    lax.fori_loop(1, count, body, 0)


def ring_hops(d):
    return min(d, 4 - d)


OFFSETS = sorted(((z, x, c) for z in range(4) for x in range(4) for c in range(2) if (z, x, c) != (0, 0, 0)),
                 key=lambda o: (-ring_hops(o[0]) - ring_hops(o[1]), -o[2]))


def star_peers(me):
    z = [lax.rem(lax.div(me, 8) + d, 4) * 8 for d in range(4)]
    x = [lax.rem(lax.div(me, 2) + d, 4) * 2 for d in range(4)]
    c = [lax.rem(me + d, 2) for d in range(2)]
    return [(z[a] + x[b] + c[d], i + 1) for i, (a, b, d) in enumerate(OFFSETS)]


def remote(src, dst, send, recv, si, gi):
    pltpu.make_async_remote_copy(src_ref=src, dst_ref=dst, send_sem=send, recv_sem=recv,
                                 device_id=(si, gi), device_id_type=MESH).start()


def kernel(star_h, knot_h, frac_h, sc_h, ac_h, cc_h, obs_h, caln_h, live,
           xs_h, xa_h, xc_h, r_h,
           star, knot, frac, sc, ac, cc, obs, caln, in_sem,
           ms, ss, ma, sa, lo7, hi6, wk, w_tab, hc, psh, psl, pat, accs, acca,
           gac, gs, rac, rs, fac, fs, halo_v, halo_r, halo_t, halo_d, halo_u, ahead,
           dac, dst, tac, tst, img_a, img_s, img, res,
           s1v, s1r, s2v, s2r,
           send_sem, ar_sem, sc_sem):
    me = lax.axis_index("stars")
    seg = lax.axis_index("seg")
    peers = star_peers(me)

    def to_stars(start):
        for p, i in peers:
            start(p, i)

    up = lax.rem(seg + 1, NG)
    down = lax.rem(seg + NG - 1, NG)

    loads = [pltpu.make_async_copy(a, b, in_sem.at[k]) for k, (a, b) in enumerate(
        ((star_h, star), (knot_h, knot), (frac_h, frac), (obs_h, obs), (caln_h, caln), (ac_h, ac), (cc_h, cc), (sc_h, sc)))]
    for c in loads:
        c.start()

    barrier = pltpu.get_barrier_semaphore()

    def hello_stars(p, i):
        pl.semaphore_signal(barrier, inc=1, device_id=(p, seg), device_id_type=MESH)

    def hello_seg(p, i):
        pl.semaphore_signal(barrier, inc=1, device_id=(me, p), device_id_type=MESH)

    to_stars(hello_stars)
    to_peers(NG, seg, hello_seg)

    for c in loads[:3]:
        c.wait()
    prepare(star, knot, frac, ms, ss, ma, sa, lo7, hi6, wk, w_tab)
    for c in loads[3:]:
        c.wait()

    mask = jnp.where(iota((128, 128), 0) < live[0], 1.0, 0.0)
    res[...] = obs[...] * mask
    hc[...] = jnp.where(iota((256, 128), 0) == jnp.broadcast_to(caln[...], (256, 128)), 1.0, 0.0).astype(BF)

    lane = iota((8, 128), 1)
    sub = iota((8, 128), 0)
    own = pl.ds(pl.multiple_of(8 * me, 8), 8)
    own_s = pl.ds(pl.multiple_of(40 * seg, 8), 40)

    def column(row, q):
        return jnp.sum(jnp.where((lane == 4 * sub + q) & (sub < 3), jnp.broadcast_to(row, (8, 128)), 0.0), axis=1, keepdims=True)

    def backward(n, val_ref, between):
        v = val_ref[...]
        for q in range(4):
            pat[q] = ac[q] * v
        acca[...] = jnp.zeros_like(acca)
        back_att(0, LOOPS, pat, ma, w_tab, acca)
        hi, lo = split(cc[...] * v)
        cal = jnp.dot(hc[...], hi, preferred_element_type=F32) + jnp.dot(hc[...], lo, preferred_element_type=F32)
        gac[n, 128:256, 0:128] = cal[0:128]
        gac[n, 128:256, 128:256] = cal[128:256]
        row = jnp.zeros((8, 128), F32)
        wide = iota((8, 256), 1)
        for q in range(4):
            x = acca[SE * q:SE * q + SE] + acca[4 * SE + SE * q:4 * SE + SE * q + SE]
            spill = x[32:40]
            over = jnp.sum(jnp.where(wide == 255, spill, 0.0), axis=1, keepdims=True)
            row = row + jnp.where((lane == 4 * sub + q) & (sub < 3), jnp.broadcast_to(over, (8, 128)), 0.0)
            row = row + jnp.where((lane == 16 + 4 * sub + q) & (sub < 3), jnp.broadcast_to(x[0:8, 0:1], (8, 128)), 0.0)
            moved = jnp.where(wide == 0, 0.0, pltpu.roll(spill, 1, 1))
            gac[n, pl.ds(32 * q, 8), :] = x[0:8] + moved
            gac[n, pl.ds(32 * q + 8, 24), :] = x[8:32]
        halo_v[n] = jnp.sum(row, axis=0, keepdims=True)
        halo_r[n, me] = halo_v[n]
        if n == 0:
            pl.semaphore_wait(barrier, NS - 1 + NG - 1)

        def send_halo(p, i):
            remote(halo_v.at[n], halo_r.at[n, me], send_sem.at[n, 0], ar_sem.at[n, 0], p, seg)

        def send_rs(p, i):
            remote(gac.at[n, pl.ds(pl.multiple_of(8 * p, 8), 8)], rac.at[n, pl.ds(8 * (i - 1), 8)],
                   send_sem.at[n, 1], ar_sem.at[n, 1], p, seg)

        to_stars(send_rs)
        to_stars(send_halo)
        between()

        for c in range(5):
            p = sc[c] * v
            h = p.astype(BF).astype(F32)
            psh[c] = h
            psl[c] = p - h
        accs[...] = jnp.zeros_like(accs)
        back_star(0, LOOPS, psh, psl, ms, ss, accs)
        gs[n] = accs[0:160] + accs[160:320]

        def send_rs_star(p, i):
            remote(gs.at[n, pl.ds(pl.multiple_of(40 * p, 8), 40)], rs.at[n, pl.ds(pl.multiple_of(40 * (i - 1), 8), 40)],
                   send_sem.at[n, 2], ar_sem.at[n, 2], me, p)

        to_peers(NG, seg, send_rs_star)

    def reduce_att(n):
        drain(rac.at[n], ar_sem.at[n, 1])
        fac[n, own, :] = tree([gac[n, own, :]] + [rac[n, 8 * i:8 * i + 8, :] for i in range(NS - 1)])

        def send_ag(p, i):
            remote(fac.at[n, own], fac.at[n, own], send_sem.at[n, 4], ar_sem.at[n, 4], p, seg)

        to_stars(send_ag)

        drain(halo_r.at[n, pl.ds(0, NS - 1)], ar_sem.at[n, 0])
        halo_t[n] = tree([halo_r[n, i] for i in range(NS)])
        remote(halo_t.at[n], halo_d.at[n], send_sem.at[n, 3], ar_sem.at[n, 3], me, up)
        remote(halo_t.at[n], halo_u.at[n], send_sem.at[n, 6], ar_sem.at[n, 6], me, down)

    def reduce_star(n):
        drain(rs.at[n], ar_sem.at[n, 2])
        fs[n, own_s, :] = gs[n, own_s, :] + rs[n, 0:40, :] + rs[n, 40:80, :] + rs[n, 80:120, :]

        def send_ag_star(p, i):
            remote(fs.at[n, own_s], fs.at[n, own_s], send_sem.at[n, 5], ar_sem.at[n, 5], me, p)

        to_peers(NG, seg, send_ag_star)

    def from_below(n):
        return jnp.where(seg > 0, halo_d[n], 0.0)

    def first_knots(n, q):
        return jnp.where(iota((8, 256), 1) == 0, jnp.broadcast_to(column(from_below(n), q), (8, 256)), 0.0)

    def halo(n, combine):
        drain(halo_d.at[n], ar_sem.at[n, 3])
        drain(halo_u.at[n], ar_sem.at[n, 6])
        t = pltpu.roll(jnp.broadcast_to(halo_u[n], (8, 128)), 112, 1)[0:1] + halo_t[n]
        ahead[n] = combine(jnp.where(seg < NG - 1, t, 0.0), ahead, slice(None))

    def own_norm(n, combine):
        mine = jnp.where((lax.rem(me, 4) == 0) & (me < 16), 1.0, 0.0)
        a = combine(fac[n, own, :] + mine * first_knots(n, me // 4), dac, own)
        s = combine(fs[n, own_s, :], dst, own_s)
        return lanes(a * a) + lanes(s * s)

    def gather_att(n, combine):
        drain(fac.at[n, pl.ds(0, 248)], ar_sem.at[n, 4])
        parts = []
        for q in range(4):
            a = pl.ds(32 * q, 8)
            b = pl.ds(32 * q + 8, 24)
            x = combine(fac[n, a, :] + first_knots(n, q), dac, a)
            y = combine(fac[n, b, :], dac, b)
            dac[n, a, :] = x
            dac[n, b, :] = y
            nb = jnp.broadcast_to(column(ahead[n], q), (8, 256))
            parts += [x, y, jnp.where(iota((8, 256), 1) == 255, nb, pltpu.roll(x, 255, 1))]
        c = pl.ds(128, 128)
        dac[n, c, :] = combine(fac[n, c, :], dac, c)
        h, l = split(jnp.concatenate(parts, axis=0))
        tac[0:4 * SE] = h
        tac[4 * SE:8 * SE] = l

    def gather_star(n, combine):
        drain(fs.at[n, pl.ds(0, 120)], ar_sem.at[n, 5])
        x = combine(fs[n], dst, slice(None))
        dst[n] = x
        h, l = split(x)
        tst[0:160] = h
        tst[160:320] = l

    def put_scalar(k, v):
        s1v[k] = v
        s1r[k, me] = v

        def send(p, i):
            remote(s1v.at[k], s1r.at[k, me], sc_sem.at[k, 0], sc_sem.at[k, 1], p, seg)

        to_stars(send)

    def mid_scalar(k):
        drain(s1r.at[k, pl.ds(0, NS - 1)], sc_sem.at[k, 1])
        t = tree([s1r[k, i] for i in range(NS)])
        s2v[k] = t
        s2r[k, seg] = t

        def send(p, i):
            remote(s2v.at[k], s2r.at[k, seg], sc_sem.at[k, 2], sc_sem.at[k, 3], me, p)

        to_peers(NG, seg, send)

    def get_scalar(k):
        drain(s2r.at[k, pl.ds(0, NG - 1)], sc_sem.at[k, 3])
        t = (s2r[k, 0] + s2r[k, 1]) + (s2r[k, 2] + s2r[k, 3])
        return jnp.sum(t, axis=1, keepdims=True)

    def lanes(x):
        t = jnp.sum(x, axis=0, keepdims=True)
        while t.shape[1] > 128:
            h = t.shape[1] // 2
            t = t[:, :h] + t[:, h:]
        return t

    def cal_image(n):
        x = dac[n, pl.ds(128, 128), :]
        x = jnp.concatenate([x[:, 0:128], x[:, 128:256]], axis=0)
        h, l = split(x)
        tn = (((0,), (0,)), ((), ()))
        v = lax.dot_general(hc[...], h, tn, preferred_element_type=F32) + lax.dot_general(hc[...], l, tn, preferred_element_type=F32)
        return cc[...] * v

    def reduce(n, combine):
        reduce_att(n)
        reduce_star(n)
        halo(n, combine)
        put_scalar(2 * n, own_norm(n, combine))

    def forward(n, combine):
        gather_att(n, combine)
        fwd_att(tac, ac, ma, w_tab, img_a)
        extra = cal_image(n)
        gather_star(n, combine)
        img_a[...] += extra
        mid_scalar(2 * n)
        fwd_star(tst, dst.at[n], sc, ms, ss, lo7, hi6, img_s)
        return (img_a[...] + img_s[...]) * jnp.where(iota((128, 128), 0) < live[0], 1.0, 0.0)

    def plain(x, ref, sl):
        return x

    backward(0, res, lambda: None)
    reduce(0, plain)
    img[...] = forward(0, plain)
    put_scalar(1, lanes(img[...] * img[...]))
    backward(1, img, lambda: mid_scalar(1))
    gg0 = get_scalar(0)
    alpha0 = gg0 / get_scalar(1)

    def step(x, ref, sl):
        return ref[0, sl] - alpha0 * x

    reduce(1, step)
    img1 = forward(1, step)
    gg1 = get_scalar(2)
    beta = gg1 / gg0
    img1 = img1 + beta * img[...]
    put_scalar(3, lanes(img1 * img1))
    res[...] = res[...] - alpha0 * img[...]
    img[...] = img1
    for n in range(2):
        drain(halo_r.at[n, pl.ds(0, NS - 1)], send_sem.at[n, 0])
        drain(rac.at[n], send_sem.at[n, 1])
        drain(rs.at[n], send_sem.at[n, 2])
        drain(halo_d.at[n], send_sem.at[n, 3])
        drain(fac.at[n, pl.ds(0, 248)], send_sem.at[n, 4])
        drain(fs.at[n, pl.ds(0, 120)], send_sem.at[n, 5])
        drain(halo_u.at[n], send_sem.at[n, 6])
    mid_scalar(3)
    alpha1 = gg1 / get_scalar(3)
    ab = alpha0 + alpha1 * beta
    res[...] = res[...] - alpha1 * img[...]
    fs[0] = ab * dst[0] + alpha1 * dst[1]
    fac[0] = ab * dac[0] + alpha1 * dac[1]
    stores = [pltpu.make_async_copy(a, b, in_sem.at[k]) for k, (a, b) in enumerate(
        ((fs.at[0], xs_h), (fac.at[0, pl.ds(0, 128)], xa_h), (fac.at[0, pl.ds(128, 128)], xc_h), (res, r_h)))]
    for c in stores:
        c.start()

    for k in range(4):
        drain(s1r.at[k, pl.ds(0, NS - 1)], sc_sem.at[k, 0])
        drain(s2r.at[k, pl.ds(0, NG - 1)], sc_sem.at[k, 2])
    for c in stores:
        c.wait()


def finish(xs_h, xa_h, xc_h, r_h, os_h, oa_h, oc_h, or_h, xs, xa, xc, r, os_, oa, oc, sem_in, sem_out):
    loads = [pltpu.make_async_copy(a, b, sem_in.at[k]) for k, (a, b) in enumerate(((xa_h, xa), (xs_h, xs), (xc_h, xc), (r_h, r)))]
    for c in loads:
        c.start()
    loads[0].wait()
    x = xa[...]
    h = x.astype(BF)
    rest = x - h.astype(F32)
    m = rest.astype(BF)
    l = (rest - m.astype(F32)).astype(BF)
    col = iota((256, 256), 1)
    pick = jnp.where(iota((256, 256), 0) == 4 * (col & 63) + (col >> 6), 1.0, 0.0).astype(BF)
    y = jnp.dot(jnp.concatenate([h, m, l], axis=0), pick, preferred_element_type=F32)
    y = (y[0:128] + y[128:256]) + y[256:384]
    for q in range(4):
        z = y[32 * q:32 * q + 32]
        a, b = z[:, 0:128], z[:, 128:256]
        t = jnp.concatenate([a, pltpu.roll(a, 64, 1), b, pltpu.roll(b, 64, 1)], axis=0).T
        for i in range(64):
            oa[q:q + 1, 128 * i:128 * i + 128] = t[i:i + 1]
    for c in loads[1:]:
        c.wait()
    for c in range(5):
        for i in range(32):
            os_[c:c + 1, 256 * i:256 * i + 256] = xs[32 * c + i:32 * c + i + 1]
    oc[0:128] = xc[:, 0:128]
    oc[128:256] = xc[:, 128:256]
    stores = [pltpu.make_async_copy(a, b, sem_out.at[k]) for k, (a, b) in enumerate(((oa, oa_h), (os_, os_h), (oc, oc_h), (r, or_h)))]
    for c in stores:
        c.start()
    for c in stores:
        c.wait()


def on_device(star, knot, frac, sc, ac, cc, tile_cal, live, obs):
    shape = jax.ShapeDtypeStruct
    T = (128, 128)
    hbm = pl.BlockSpec(memory_space=pl.ANY)
    V = pltpu.VMEM
    sem = pltpu.SemaphoreType.DMA
    parts = pl.pallas_call(
        kernel,
        in_specs=[hbm] * 8 + [pl.BlockSpec(memory_space=pltpu.SMEM)],
        out_specs=[hbm] * 4,
        out_shape=[shape((160, 256), F32), shape((128, 256), F32), shape((128, 256), F32), shape(T, F32)],
        scratch_shapes=[
            V(T, jnp.int32), V(T, jnp.int32), V(T, F32), V((5,) + T, F32), V((4,) + T, F32), V(T, F32), V(T, F32),
            V((1, 128), jnp.int32), sem((8,)),
            V(T, F32), V(T, F32), V(T, F32), V(T, jnp.int32), V((ROWS, 128), jnp.int32), V((ROWS, 128), jnp.int32), V((4,) + T, F32), V((128, SE, 128), F32),
            V((256, 128), BF), V((5,) + T, F32), V((5,) + T, F32), V((4,) + T, F32), V((320, 256), F32), V((320, 256), F32),
            V((2, 256, 256), F32), V((2, 160, 256), F32), V((2, 248, 256), F32), V((2, 120, 256), F32),
            V((2, 256, 256), F32), V((2, 160, 256), F32),
            V((2, 1, 128), F32), V((2, NS, 1, 128), F32), V((2, 1, 128), F32), V((2, 1, 128), F32), V((2, 1, 128), F32), V((2, 1, 128), F32),
            V((2, 256, 256), F32), V((2, 160, 256), F32), V((320, 256), BF), V((320, 256), BF),
            V(T, F32), V(T, F32), V(T, F32), V(T, F32),
            V((4, 1, 128), F32), V((4, NS, 1, 128), F32), V((4, 1, 128), F32), V((4, NG, 1, 128), F32),
            sem((2, 7)), sem((2, 7)), sem((4, 4)),
        ],
        compiler_params=pltpu.CompilerParams(collective_id=0, has_side_effects=True, vmem_limit_bytes=60 << 20),
        name="solve",
    )(star, knot, frac, sc, ac, cc, obs, tile_cal.reshape(1, 128), live)
    return pl.pallas_call(
        finish,
        in_specs=[hbm] * 4,
        out_specs=[hbm] * 4,
        out_shape=[shape((5, 8192), F32), shape((4, 8192), F32), shape((256, 128), F32), shape(T, F32)],
        scratch_shapes=[V((160, 256), F32), V((128, 256), F32), V((128, 256), F32), V(T, F32),
                        V((5, 8192), F32), V((4, 8192), F32), V((256, 128), F32), sem((4,)), sem((4,))],
        compiler_params=pltpu.CompilerParams(vmem_limit_bytes=60 << 20),
        name="finish",
    )(*parts)


def solution(mesh):
    P = jax.sharding.PartitionSpec
    a = P(("stars", "seg"), None)
    b = P(None, ("stars", "seg"), None)
    c = P(("stars", "seg"))
    return jax.shard_map(on_device, mesh=mesh, in_specs=(a, a, a, b, b, a, c, c, a),
                         out_specs=(P(None, "stars"), P(None, "seg"), P("seg", None), a), check_vma=False)
```

```python
import jax
import jax.numpy as jnp
from jax import lax
from jax.experimental import pallas as pl
from jax.experimental.pallas import tpu as pltpu

BF = jnp.bfloat16
F32 = jnp.float32
SE = 40
U = 32
LOOPS = 128 // U
ROWS = 48
SLOOPS = 2
STEP = (128 - ROWS) // SLOOPS
ALOOPS = 2
AROWS = 48
ASTEP = (128 - AROWS) // ALOOPS
NS = 32
NG = 4
MESH = pl.DeviceIdType.MESH


def split(x):
    hi = x.astype(BF)
    return hi, (x - hi.astype(F32)).astype(BF)


def row16(ref, t):
    return jnp.broadcast_to(ref[pl.ds(t, 1), :], (16, 128)).astype(BF)


def iota16():
    return lax.broadcasted_iota(jnp.int32, (16, 128), 0).astype(F32).astype(BF)


def onehot(ref, t, n):
    r = row16(ref, t)
    i = iota16()
    one = jnp.ones((16, 128), BF)
    zero = jnp.zeros((16, 128), BF)
    return jnp.concatenate([jnp.where(i + BF(16 * k) == r, one, zero) for k in range(n // 16)], axis=0)


def iota(shape, axis):
    return lax.broadcasted_iota(jnp.int32, shape, axis)


def prepare(star, knot, frac, ms, ss, ma, sa, lo7, hi6, alo, ahi, wk, w_tab):
    s = star[...]
    k = knot[...]
    ms[...] = (s & 255).astype(F32)
    ss[...] = (s >> 8).astype(F32)
    ma[...] = (k >> 5).astype(F32)
    sa[...] = k & 31
    lo7[...] = s[0:ROWS] & 127
    hi6[...] = s[0:ROWS] >> 7
    alo[...] = (k[0:AROWS] >> 5) & 127
    ahi[...] = k[0:AROWS] >> 12
    u = frac[...]
    rem = 1.0 - u
    sq = u * u
    cu = sq * u
    wk[0] = rem * rem * rem / 6.0
    wk[1] = (3.0 * cu - 6.0 * sq + 4.0) / 6.0
    wk[2] = (-3.0 * cu + 3.0 * sq + 3.0 * u + 1.0) / 6.0
    wk[3] = cu / 6.0

    def body(b, _):
        for u in range(8):
            t = b * 8 + u
            kk = jnp.broadcast_to(sa[pl.ds(t, 1), :], (8, 128))
            w = [jnp.broadcast_to(wk[j, pl.ds(t, 1), :], (8, 128)) for j in range(4)]
            base = iota((8, 128), 0) - kk
            for j in range(SE // 8):
                d = base + 8 * j
                v = jnp.where(d == 0, w[0], jnp.where(d == 1, w[1], jnp.where(d == 2, w[2], jnp.where(d == 3, w[3], 0.0))))
                w_tab[t, pl.ds(8 * j, 8), :] = v
        return 0

    lax.fori_loop(0, 16, body, 0)


DN = (((1,), (1,)), ((), ()))


def back_att(start, stop, pat, ma, w_tab, acc):
    def body(b, _):
        hs = []
        rows = []
        for u in range(U):
            t = b * U + u
            hs.append(onehot(ma, t, 256))
            w = w_tab[t]
            a = jnp.concatenate([w * jnp.broadcast_to(pat[q, pl.ds(t, 1), :], (SE, 128)) for q in range(4)], axis=0)
            h, l = split(a)
            rows.append(jnp.concatenate([h, l], axis=0))
        acc[...] += lax.dot_general(jnp.concatenate(rows, 1), jnp.concatenate(hs, 1), DN, preferred_element_type=F32)
        return 0

    lax.fori_loop(start, stop, body, 0)


def back_star(start, stop, psh, psl, ms, ss, acc):
    z16 = jnp.zeros((16, 128), BF)

    def body(b, _):
        hs = []
        rows = []
        for u in range(U):
            t = b * U + u
            hs.append(onehot(ms, t, 256))
            r = row16(ss, t)
            i = iota16()
            masks = [(i + BF(16 * k)) == r for k in range(2)]
            his = []
            los = []
            for c in range(5):
                h = row16(psh.at[c], t)
                l = row16(psl.at[c], t)
                his += [jnp.where(m, h, z16) for m in masks]
                los += [jnp.where(m, l, z16) for m in masks]
            rows.append(jnp.concatenate(his + los, axis=0))
        acc[...] += lax.dot_general(jnp.concatenate(rows, 1), jnp.concatenate(hs, 1), DN, preferred_element_type=F32)
        return 0

    lax.fori_loop(start, stop, body, 0)


def fwd_star(tab, full, sc, ms, ss, lo7, hi6, out):
    i8 = iota((8, 128), 0).astype(F32)

    def body(b, _):
        base = ROWS + b * STEP
        h = jnp.concatenate([onehot(ms, base + u, 256) for u in range(STEP)], 1)
        x = jnp.dot(tab[...], h, preferred_element_type=F32)
        for k in range(ROWS // 8 // SLOOPS):
            r0 = pl.ds(pl.multiple_of((b * (ROWS // 8 // SLOOPS) + k) * 8, 8), 8)
            lo = lo7[r0, :]
            hi = hi6[r0, :]
            acc = [jnp.zeros((8, 128), F32)] * 5
            for r in range(64):
                m = hi == r
                for c in range(5):
                    t = full[32 * c + r // 2:32 * c + r // 2 + 1, 128 * (r % 2):128 * (r % 2) + 128]
                    t = jnp.take_along_axis(jnp.broadcast_to(t, (8, 128)), lo, axis=1)
                    acc[c] = jnp.where(m, t, acc[c])
            t = acc[0] * sc[0, r0, :]
            for c in range(1, 5):
                t = t + acc[c] * sc[c, r0, :]
            out[r0, :] = t
        rows = []
        for u in range(STEP):
            t = base + u
            sl = slice(128 * u, 128 * u + 128)
            g = None
            for c in range(5):
                y = (x[32 * c:32 * c + 32, sl] + x[160 + 32 * c:192 + 32 * c, sl]) * jnp.broadcast_to(sc[c, pl.ds(t, 1), :], (32, 128))
                g = y if g is None else g + y
            s = jnp.broadcast_to(ss[pl.ds(t, 1), :], (8, 128))
            tot = None
            for j in range(4):
                y = jnp.where(i8 + 8.0 * j == s, g[8 * j:8 * j + 8], 0.0)
                tot = y if tot is None else tot + y
            rows.append(jnp.sum(tot, axis=0, keepdims=True))
        out[pl.ds(pl.multiple_of(base, 8), STEP), :] = jnp.concatenate(rows, 0)
        return 0

    lax.fori_loop(0, SLOOPS, body, 0)


def fwd_att(tab, full, ac, ma, w_tab, alo, ahi, sa, wk, out):
    def body(b, _):
        base = AROWS + b * ASTEP
        h = jnp.concatenate([onehot(ma, base + u, 256) for u in range(ASTEP)], 1)
        x = jnp.dot(tab[...], h, preferred_element_type=F32)
        groups = AROWS // 8 // ALOOPS
        for k in range(groups):
            r0 = pl.ds(pl.multiple_of((b * groups + k) * 8, 8), 8)
            lo = alo[r0, :]
            upper = ahi[r0, :] == 1
            s = sa[r0, :]
            w = [wk[j, r0, :] for j in range(4)]
            acc = [jnp.zeros((8, 128), F32)] * 4
            for r in range(35):
                v = jnp.zeros((8, 128), F32)
                for j in range(4):
                    if 0 <= r - j < 32:
                        v = jnp.where(s == r - j, w[j], v)
                for q in range(4):
                    t = [jnp.take_along_axis(jnp.broadcast_to(full[SE * q + r:SE * q + r + 1, a:a + 128], (8, 128)), lo, axis=1)
                         for a in (0, 128)]
                    acc[q] = acc[q] + v * jnp.where(upper, t[1], t[0])
            t = acc[0] * ac[0, r0, :]
            for q in range(1, 4):
                t = t + acc[q] * ac[q, r0, :]
            out[r0, :] = t
        rows = []
        for u in range(ASTEP):
            t = base + u
            sl = slice(128 * u, 128 * u + 128)
            g = None
            for q in range(4):
                y = (x[SE * q:SE * q + SE, sl] + x[4 * SE + SE * q:4 * SE + SE * q + SE, sl]) * jnp.broadcast_to(ac[q, pl.ds(t, 1), :], (SE, 128))
                g = y if g is None else g + y
            g = g * w_tab[t]
            tot = None
            for j in range(SE // 8):
                y = g[8 * j:8 * j + 8]
                tot = y if tot is None else tot + y
            rows.append(jnp.sum(tot, axis=0, keepdims=True))
        out[pl.ds(pl.multiple_of(base, 8), ASTEP), :] = jnp.concatenate(rows, 0)
        return 0

    lax.fori_loop(0, ALOOPS, body, 0)


def tree(xs):
    while len(xs) > 1:
        xs = [a + b for a, b in zip(xs[::2], xs[1::2])]
    return xs[0]


def drain(ref, sem):
    pltpu.make_async_copy(ref, ref, sem).wait()


def to_peers(count, me, start):
    def body(i, _):
        start(lax.rem(me + i, count), i)
        return 0

    lax.fori_loop(1, count, body, 0)


def ring_hops(d):
    return min(d, 4 - d)


OFFSETS = sorted(((z, x, c) for z in range(4) for x in range(4) for c in range(2) if (z, x, c) != (0, 0, 0)),
                 key=lambda o: (-ring_hops(o[0]) - ring_hops(o[1]), -o[2]))


def star_peers(me):
    z = [lax.rem(lax.div(me, 8) + d, 4) * 8 for d in range(4)]
    x = [lax.rem(lax.div(me, 2) + d, 4) * 2 for d in range(4)]
    c = [lax.rem(me + d, 2) for d in range(2)]
    return [(z[a] + x[b] + c[d], i + 1) for i, (a, b, d) in enumerate(OFFSETS)]


def remote(src, dst, send, recv, si, gi):
    pltpu.make_async_remote_copy(src_ref=src, dst_ref=dst, send_sem=send, recv_sem=recv,
                                 device_id=(si, gi), device_id_type=MESH).start()


def kernel(star_h, knot_h, frac_h, sc_h, ac_h, cc_h, obs_h, caln_h, live,
           xs_h, xa_h, xc_h, r_h,
           star, knot, frac, sc, ac, cc, obs, caln, in_sem,
           ms, ss, ma, sa, lo7, hi6, alo, ahi, wk, w_tab, hc, psh, psl, pat, accs, acca,
           gac, gs, rac, rs, fac, fs, halo_v, halo_r, halo_t, halo_d, halo_u, ahead,
           dac, dst, tac, tax, tst, img_a, img_s, img, res,
           s1v, s1r, s2v, s2r, ls, la, oc,
           send_sem, ar_sem, sc_sem):
    me = lax.axis_index("stars")
    seg = lax.axis_index("seg")
    peers = star_peers(me)

    def to_stars(start):
        for p, i in peers:
            start(p, i)

    up = lax.rem(seg + 1, NG)
    down = lax.rem(seg + NG - 1, NG)

    loads = [pltpu.make_async_copy(a, b, in_sem.at[k]) for k, (a, b) in enumerate(
        ((star_h, star), (knot_h, knot), (frac_h, frac), (obs_h, obs), (caln_h, caln), (ac_h, ac), (cc_h, cc), (sc_h, sc)))]
    for c in loads:
        c.start()

    barrier = pltpu.get_barrier_semaphore()

    def hello_stars(p, i):
        pl.semaphore_signal(barrier, inc=1, device_id=(p, seg), device_id_type=MESH)

    def hello_seg(p, i):
        pl.semaphore_signal(barrier, inc=1, device_id=(me, p), device_id_type=MESH)

    to_stars(hello_stars)
    to_peers(NG, seg, hello_seg)

    for c in loads[:3]:
        c.wait()
    prepare(star, knot, frac, ms, ss, ma, sa, lo7, hi6, alo, ahi, wk, w_tab)
    for c in loads[3:]:
        c.wait()

    mask = jnp.where(iota((128, 128), 0) < live[0], 1.0, 0.0)
    res[...] = obs[...] * mask
    hc[...] = jnp.where(iota((256, 128), 0) == jnp.broadcast_to(caln[...], (256, 128)), 1.0, 0.0).astype(BF)

    lane = iota((8, 128), 1)
    sub = iota((8, 128), 0)
    own = pl.ds(pl.multiple_of(8 * me, 8), 8)
    own_s = pl.ds(pl.multiple_of(40 * seg, 8), 40)

    def column(row, q):
        return jnp.sum(jnp.where((lane == 4 * sub + q) & (sub < 3), jnp.broadcast_to(row, (8, 128)), 0.0), axis=1, keepdims=True)

    def backward(n, val_ref, between):
        v = val_ref[...]
        for q in range(4):
            pat[q] = ac[q] * v
        acca[...] = jnp.zeros_like(acca)
        back_att(0, LOOPS, pat, ma, w_tab, acca)
        hi, lo = split(cc[...] * v)
        cal = jnp.dot(hc[...], hi, preferred_element_type=F32) + jnp.dot(hc[...], lo, preferred_element_type=F32)
        gac[n, 128:256, 0:128] = cal[0:128]
        gac[n, 128:256, 128:256] = cal[128:256]
        row = jnp.zeros((8, 128), F32)
        wide = iota((8, 256), 1)
        for q in range(4):
            x = acca[SE * q:SE * q + SE] + acca[4 * SE + SE * q:4 * SE + SE * q + SE]
            spill = x[32:40]
            over = jnp.sum(jnp.where(wide == 255, spill, 0.0), axis=1, keepdims=True)
            row = row + jnp.where((lane == 4 * sub + q) & (sub < 3), jnp.broadcast_to(over, (8, 128)), 0.0)
            row = row + jnp.where((lane == 16 + 4 * sub + q) & (sub < 3), jnp.broadcast_to(x[0:8, 0:1], (8, 128)), 0.0)
            moved = jnp.where(wide == 0, 0.0, pltpu.roll(spill, 1, 1))
            gac[n, pl.ds(32 * q, 8), :] = x[0:8] + moved
            gac[n, pl.ds(32 * q + 8, 24), :] = x[8:32]
        halo_v[n] = jnp.sum(row, axis=0, keepdims=True)
        halo_r[n, me] = halo_v[n]
        if n == 0:
            pl.semaphore_wait(barrier, NS - 1 + NG - 1)

        def send_halo(p, i):
            remote(halo_v.at[n], halo_r.at[n, me], send_sem.at[n, 0], ar_sem.at[n, 0], p, seg)

        def send_rs(p, i):
            remote(gac.at[n, pl.ds(pl.multiple_of(8 * p, 8), 8)], rac.at[n, pl.ds(8 * (i - 1), 8)],
                   send_sem.at[n, 1], ar_sem.at[n, 1], p, seg)

        to_stars(send_rs)
        to_stars(send_halo)
        between()

        for c in range(5):
            p = sc[c] * v
            h = p.astype(BF).astype(F32)
            psh[c] = h
            psl[c] = p - h
        accs[...] = jnp.zeros_like(accs)
        back_star(0, LOOPS, psh, psl, ms, ss, accs)
        gs[n] = accs[0:160] + accs[160:320]

        def send_rs_star(p, i):
            remote(gs.at[n, pl.ds(pl.multiple_of(40 * p, 8), 40)], rs.at[n, pl.ds(pl.multiple_of(40 * (i - 1), 8), 40)],
                   send_sem.at[n, 2], ar_sem.at[n, 2], me, p)

        to_peers(NG, seg, send_rs_star)

    def reduce_att(n):
        drain(rac.at[n], ar_sem.at[n, 1])
        fac[n, own, :] = tree([gac[n, own, :]] + [rac[n, 8 * i:8 * i + 8, :] for i in range(NS - 1)])

        def send_ag(p, i):
            remote(fac.at[n, own], fac.at[n, own], send_sem.at[n, 4], ar_sem.at[n, 4], p, seg)

        to_stars(send_ag)

        drain(halo_r.at[n, pl.ds(0, NS - 1)], ar_sem.at[n, 0])
        halo_t[n] = tree([halo_r[n, i] for i in range(NS)])
        remote(halo_t.at[n], halo_d.at[n], send_sem.at[n, 3], ar_sem.at[n, 3], me, up)
        remote(halo_t.at[n], halo_u.at[n], send_sem.at[n, 6], ar_sem.at[n, 6], me, down)

    def reduce_star(n):
        drain(rs.at[n], ar_sem.at[n, 2])
        fs[n, own_s, :] = gs[n, own_s, :] + rs[n, 0:40, :] + rs[n, 40:80, :] + rs[n, 80:120, :]

        def send_ag_star(p, i):
            remote(fs.at[n, own_s], fs.at[n, own_s], send_sem.at[n, 5], ar_sem.at[n, 5], me, p)

        to_peers(NG, seg, send_ag_star)

    def from_below(n):
        return jnp.where(seg > 0, halo_d[n], 0.0)

    def first_knots(n, q):
        return jnp.where(iota((8, 256), 1) == 0, jnp.broadcast_to(column(from_below(n), q), (8, 256)), 0.0)

    def halo(n, combine):
        drain(halo_d.at[n], ar_sem.at[n, 3])
        drain(halo_u.at[n], ar_sem.at[n, 6])
        t = pltpu.roll(jnp.broadcast_to(halo_u[n], (8, 128)), 112, 1)[0:1] + halo_t[n]
        ahead[n] = combine(jnp.where(seg < NG - 1, t, 0.0), ahead, slice(None))

    def own_norm(n, combine):
        mine = jnp.where((lax.rem(me, 4) == 0) & (me < 16), 1.0, 0.0)
        a = combine(fac[n, own, :] + mine * first_knots(n, me // 4), dac, own)
        s = combine(fs[n, own_s, :], dst, own_s)
        return lanes(a * a) + lanes(s * s)

    def gather_att(n, combine):
        drain(fac.at[n, pl.ds(0, 248)], ar_sem.at[n, 4])
        parts = []
        for q in range(4):
            a = pl.ds(32 * q, 8)
            b = pl.ds(32 * q + 8, 24)
            x = combine(fac[n, a, :] + first_knots(n, q), dac, a)
            y = combine(fac[n, b, :], dac, b)
            dac[n, a, :] = x
            dac[n, b, :] = y
            nb = jnp.broadcast_to(column(ahead[n], q), (8, 256))
            parts += [x, y, jnp.where(iota((8, 256), 1) == 255, nb, pltpu.roll(x, 255, 1))]
        c = pl.ds(128, 128)
        dac[n, c, :] = combine(fac[n, c, :], dac, c)
        tax[...] = jnp.concatenate(parts, axis=0)
        h, l = split(tax[...])
        tac[0:4 * SE] = h
        tac[4 * SE:8 * SE] = l

    def gather_star(n, combine):
        drain(fs.at[n, pl.ds(0, 120)], ar_sem.at[n, 5])
        x = combine(fs[n], dst, slice(None))
        dst[n] = x
        h, l = split(x)
        tst[0:160] = h
        tst[160:320] = l

    def put_scalar(k, v):
        s1v[k] = v
        s1r[k, me] = v

        def send(p, i):
            remote(s1v.at[k], s1r.at[k, me], sc_sem.at[k, 0], sc_sem.at[k, 1], p, seg)

        to_stars(send)

    def mid_scalar(k):
        drain(s1r.at[k, pl.ds(0, NS - 1)], sc_sem.at[k, 1])
        t = tree([s1r[k, i] for i in range(NS)])
        s2v[k] = t
        s2r[k, seg] = t

        def send(p, i):
            remote(s2v.at[k], s2r.at[k, seg], sc_sem.at[k, 2], sc_sem.at[k, 3], me, p)

        to_peers(NG, seg, send)

    def get_scalar(k):
        drain(s2r.at[k, pl.ds(0, NG - 1)], sc_sem.at[k, 3])
        t = (s2r[k, 0] + s2r[k, 1]) + (s2r[k, 2] + s2r[k, 3])
        return jnp.sum(t, axis=1, keepdims=True)

    def lanes(x):
        t = jnp.sum(x, axis=0, keepdims=True)
        while t.shape[1] > 128:
            h = t.shape[1] // 2
            t = t[:, :h] + t[:, h:]
        return t

    def cal_image(n):
        x = dac[n, pl.ds(128, 128), :]
        x = jnp.concatenate([x[:, 0:128], x[:, 128:256]], axis=0)
        h, l = split(x)
        tn = (((0,), (0,)), ((), ()))
        v = lax.dot_general(hc[...], h, tn, preferred_element_type=F32) + lax.dot_general(hc[...], l, tn, preferred_element_type=F32)
        return cc[...] * v

    def reduce(n, combine):
        reduce_att(n)
        reduce_star(n)
        halo(n, combine)
        put_scalar(2 * n, own_norm(n, combine))

    def forward(n, combine):
        gather_att(n, combine)
        fwd_att(tac, tax, ac, ma, w_tab, alo, ahi, sa, wk, img_a)
        extra = cal_image(n)
        gather_star(n, combine)
        img_a[...] += extra
        mid_scalar(2 * n)
        fwd_star(tst, dst.at[n], sc, ms, ss, lo7, hi6, img_s)
        return (img_a[...] + img_s[...]) * jnp.where(iota((128, 128), 0) < live[0], 1.0, 0.0)

    def lay_out(n):
        x = dac[n, 0:128]
        h = x.astype(BF)
        rest = x - h.astype(F32)
        m = rest.astype(BF)
        l = (rest - m.astype(F32)).astype(BF)
        col = iota((256, 256), 1)
        pick = jnp.where(iota((256, 256), 0) == 4 * (col & 63) + (col >> 6), 1.0, 0.0).astype(BF)
        y = jnp.dot(jnp.concatenate([h, m, l], axis=0), pick, preferred_element_type=F32)
        y = (y[0:128] + y[128:256]) + y[256:384]
        for q in range(4):
            z = y[32 * q:32 * q + 32]
            a, b = z[:, 0:128], z[:, 128:256]
            t = jnp.concatenate([a, pltpu.roll(a, 64, 1), b, pltpu.roll(b, 64, 1)], axis=0).T
            for i in range(64):
                la[n, q:q + 1, 128 * i:128 * i + 128] = t[i:i + 1]
        for c in range(5):
            for i in range(32):
                ls[n, c:c + 1, 256 * i:256 * i + 256] = dst[n, 32 * c + i:32 * c + i + 1]

    def plain(x, ref, sl):
        return x

    backward(0, res, lambda: None)
    reduce(0, plain)
    img[...] = forward(0, plain)
    put_scalar(1, lanes(img[...] * img[...]))
    backward(1, img, lambda: mid_scalar(1))
    gg0 = get_scalar(0)
    alpha0 = gg0 / get_scalar(1)

    def step(x, ref, sl):
        return ref[0, sl] - alpha0 * x

    reduce(1, step)
    lay_out(0)
    img1 = forward(1, step)
    gg1 = get_scalar(2)
    beta = gg1 / gg0
    img1 = img1 + beta * img[...]
    put_scalar(3, lanes(img1 * img1))
    lay_out(1)
    oc[0, 0:128] = dac[0, 128:256, 0:128]
    oc[0, 128:256] = dac[0, 128:256, 128:256]
    oc[1, 0:128] = dac[1, 128:256, 0:128]
    oc[1, 128:256] = dac[1, 128:256, 128:256]
    res[...] = res[...] - alpha0 * img[...]
    img[...] = img1
    for n in range(2):
        drain(halo_r.at[n, pl.ds(0, NS - 1)], send_sem.at[n, 0])
        drain(rac.at[n], send_sem.at[n, 1])
        drain(rs.at[n], send_sem.at[n, 2])
        drain(halo_d.at[n], send_sem.at[n, 3])
        drain(fac.at[n, pl.ds(0, 248)], send_sem.at[n, 4])
        drain(fs.at[n, pl.ds(0, 120)], send_sem.at[n, 5])
        drain(halo_u.at[n], send_sem.at[n, 6])
    mid_scalar(3)
    alpha1 = gg1 / get_scalar(3)
    ab = alpha0 + alpha1 * beta
    res[...] = res[...] - alpha1 * img[...]
    for o in (ls, la, oc):
        o[0] = ab * o[0] + alpha1 * o[1]
    stores = [pltpu.make_async_copy(a, b, in_sem.at[k]) for k, (a, b) in enumerate(
        ((ls.at[0], xs_h), (la.at[0], xa_h), (oc.at[0], xc_h), (res, r_h)))]
    for c in stores:
        c.start()

    for k in range(4):
        drain(s1r.at[k, pl.ds(0, NS - 1)], sc_sem.at[k, 0])
        drain(s2r.at[k, pl.ds(0, NG - 1)], sc_sem.at[k, 2])
    for c in stores:
        c.wait()


def finish(a, b, c, d, ao, bo, co, do, av, bv, cv, dv, sem_in, sem_out):
    loads = [pltpu.make_async_copy(x, y, sem_in.at[k]) for k, (x, y) in enumerate(((a, av), (b, bv), (c, cv), (d, dv)))]
    stores = [pltpu.make_async_copy(x, y, sem_out.at[k]) for k, (x, y) in enumerate(((av, ao), (bv, bo), (cv, co), (dv, do)))]
    for x in loads:
        x.start()
    for x, y in zip(loads, stores):
        x.wait()
        y.start()
    for y in stores:
        y.wait()


def on_device(star, knot, frac, sc, ac, cc, tile_cal, live, obs):
    shape = jax.ShapeDtypeStruct
    T = (128, 128)
    hbm = pl.BlockSpec(memory_space=pl.ANY)
    V = pltpu.VMEM
    sem = pltpu.SemaphoreType.DMA
    outs = [shape((5, 8192), F32), shape((4, 8192), F32), shape((256, 128), F32), shape(T, F32)]
    parts = pl.pallas_call(
        kernel,
        in_specs=[hbm] * 8 + [pl.BlockSpec(memory_space=pltpu.SMEM)],
        out_specs=[hbm] * 4,
        out_shape=outs,
        scratch_shapes=[
            V(T, jnp.int32), V(T, jnp.int32), V(T, F32), V((5,) + T, F32), V((4,) + T, F32), V(T, F32), V(T, F32),
            V((1, 128), jnp.int32), sem((8,)),
            V(T, F32), V(T, F32), V(T, F32), V(T, jnp.int32), V((ROWS, 128), jnp.int32), V((ROWS, 128), jnp.int32), V((AROWS, 128), jnp.int32), V((AROWS, 128), jnp.int32), V((4,) + T, F32), V((128, SE, 128), F32),
            V((256, 128), BF), V((5,) + T, F32), V((5,) + T, F32), V((4,) + T, F32), V((320, 256), F32), V((320, 256), F32),
            V((2, 256, 256), F32), V((2, 160, 256), F32), V((2, 248, 256), F32), V((2, 120, 256), F32),
            V((2, 256, 256), F32), V((2, 160, 256), F32),
            V((2, 1, 128), F32), V((2, NS, 1, 128), F32), V((2, 1, 128), F32), V((2, 1, 128), F32), V((2, 1, 128), F32), V((2, 1, 128), F32),
            V((2, 256, 256), F32), V((2, 160, 256), F32), V((320, 256), BF), V((160, 256), F32), V((320, 256), BF),
            V(T, F32), V(T, F32), V(T, F32), V(T, F32),
            V((4, 1, 128), F32), V((4, NS, 1, 128), F32), V((4, 1, 128), F32), V((4, NG, 1, 128), F32),
            V((2, 5, 8192), F32), V((2, 4, 8192), F32), V((2, 256, 128), F32),
            sem((2, 7)), sem((2, 7)), sem((4, 4)),
        ],
        compiler_params=pltpu.CompilerParams(collective_id=0, has_side_effects=True, vmem_limit_bytes=60 << 20),
        name="solve",
    )(star, knot, frac, sc, ac, cc, obs, tile_cal.reshape(1, 128), live)
    return pl.pallas_call(
        finish,
        in_specs=[hbm] * 4,
        out_specs=[hbm] * 4,
        out_shape=outs,
        scratch_shapes=[V(o.shape, F32) for o in outs] + [sem((4,)), sem((4,))],
        compiler_params=pltpu.CompilerParams(vmem_limit_bytes=60 << 20),
        name="finish",
    )(*parts)


def solution(mesh):
    P = jax.sharding.PartitionSpec
    a = P(("stars", "seg"), None)
    b = P(None, ("stars", "seg"), None)
    c = P(("stars", "seg"))
    return jax.shard_map(on_device, mesh=mesh, in_specs=(a, a, a, b, b, a, c, c, a),
                         out_specs=(P(None, "stars"), P(None, "seg"), P("seg", None), a), check_vma=False)
```

```python
import jax
import jax.numpy as jnp
from jax import lax
from jax.experimental import pallas as pl
from jax.experimental.pallas import tpu as pltpu

BF = jnp.bfloat16
F32 = jnp.float32
SE = 40
U = 64
LOOPS = 128 // U
ROWS = 48
SLOOPS = 2
STEP = (128 - ROWS) // SLOOPS
ALOOPS = 2
AROWS = 48
ASTEP = (128 - AROWS) // ALOOPS
NS = 32
NG = 4
MESH = pl.DeviceIdType.MESH


def split(x):
    hi = x.astype(BF)
    return hi, (x - hi.astype(F32)).astype(BF)


def row16(ref, t):
    return jnp.broadcast_to(ref[pl.ds(t, 1), :], (16, 128)).astype(BF)


def iota16():
    return lax.broadcasted_iota(jnp.int32, (16, 128), 0).astype(F32).astype(BF)


def onehot(ref, t, n):
    r = row16(ref, t)
    i = iota16()
    one = jnp.ones((16, 128), BF)
    zero = jnp.zeros((16, 128), BF)
    return jnp.concatenate([jnp.where(i + BF(16 * k) == r, one, zero) for k in range(n // 16)], axis=0)


def iota(shape, axis):
    return lax.broadcasted_iota(jnp.int32, shape, axis)


def prepare(star, knot, frac, ms, ss, ma, sa, lo7, hi6, alo, ahi, wk, w_tab):
    s = star[...]
    k = knot[...]
    ms[...] = (s & 255).astype(F32)
    ss[...] = (s >> 8).astype(F32)
    ma[...] = (k >> 5).astype(F32)
    sa[...] = k & 31
    lo7[...] = s[0:ROWS] & 127
    hi6[...] = s[0:ROWS] >> 7
    alo[...] = (k[0:AROWS] >> 5) & 127
    ahi[...] = k[0:AROWS] >> 12
    u = frac[...]
    rem = 1.0 - u
    sq = u * u
    cu = sq * u
    wk[0] = rem * rem * rem / 6.0
    wk[1] = (3.0 * cu - 6.0 * sq + 4.0) / 6.0
    wk[2] = (-3.0 * cu + 3.0 * sq + 3.0 * u + 1.0) / 6.0
    wk[3] = cu / 6.0

    def body(b, _):
        for u in range(8):
            t = b * 8 + u
            kk = jnp.broadcast_to(sa[pl.ds(t, 1), :], (8, 128))
            w = [jnp.broadcast_to(wk[j, pl.ds(t, 1), :], (8, 128)) for j in range(4)]
            base = iota((8, 128), 0) - kk
            for j in range(SE // 8):
                d = base + 8 * j
                v = jnp.where(d == 0, w[0], jnp.where(d == 1, w[1], jnp.where(d == 2, w[2], jnp.where(d == 3, w[3], 0.0))))
                w_tab[t, pl.ds(8 * j, 8), :] = v
        return 0

    lax.fori_loop(0, 16, body, 0)


DN = (((1,), (1,)), ((), ()))


def back_att(start, stop, pat, ma, w_tab, acc):
    def body(b, _):
        hs = []
        rows = []
        for u in range(U):
            t = b * U + u
            hs.append(onehot(ma, t, 256))
            w = w_tab[t]
            a = jnp.concatenate([w * jnp.broadcast_to(pat[q, pl.ds(t, 1), :], (SE, 128)) for q in range(4)], axis=0)
            h, l = split(a)
            rows.append(jnp.concatenate([h, l], axis=0))
        acc[...] += lax.dot_general(jnp.concatenate(rows, 1), jnp.concatenate(hs, 1), DN, preferred_element_type=F32)
        return 0

    lax.fori_loop(start, stop, body, 0)


def back_star(start, stop, psh, psl, ms, ss, acc):
    z16 = jnp.zeros((16, 128), BF)

    def body(b, _):
        hs = []
        rows = []
        for u in range(U):
            t = b * U + u
            hs.append(onehot(ms, t, 256))
            r = row16(ss, t)
            i = iota16()
            masks = [(i + BF(16 * k)) == r for k in range(2)]
            his = []
            los = []
            for c in range(5):
                h = row16(psh.at[c], t)
                l = row16(psl.at[c], t)
                his += [jnp.where(m, h, z16) for m in masks]
                los += [jnp.where(m, l, z16) for m in masks]
            rows.append(jnp.concatenate(his + los, axis=0))
        acc[...] += lax.dot_general(jnp.concatenate(rows, 1), jnp.concatenate(hs, 1), DN, preferred_element_type=F32)
        return 0

    lax.fori_loop(start, stop, body, 0)


def fwd_star(tab, full, sc, ms, ss, lo7, hi6, out):
    i8 = iota((8, 128), 0).astype(F32)

    def body(b, _):
        base = ROWS + b * STEP
        h = jnp.concatenate([onehot(ms, base + u, 256) for u in range(STEP)], 1)
        x = jnp.dot(tab[...], h, preferred_element_type=F32)
        for k in range(ROWS // 8 // SLOOPS):
            r0 = pl.ds(pl.multiple_of((b * (ROWS // 8 // SLOOPS) + k) * 8, 8), 8)
            lo = lo7[r0, :]
            hi = hi6[r0, :]
            acc = [jnp.zeros((8, 128), F32)] * 5
            for r in range(64):
                m = hi == r
                for c in range(5):
                    t = full[32 * c + r // 2:32 * c + r // 2 + 1, 128 * (r % 2):128 * (r % 2) + 128]
                    t = jnp.take_along_axis(jnp.broadcast_to(t, (8, 128)), lo, axis=1)
                    acc[c] = jnp.where(m, t, acc[c])
            t = acc[0] * sc[0, r0, :]
            for c in range(1, 5):
                t = t + acc[c] * sc[c, r0, :]
            out[r0, :] = t
        rows = []
        for u in range(STEP):
            t = base + u
            sl = slice(128 * u, 128 * u + 128)
            g = None
            for c in range(5):
                y = (x[32 * c:32 * c + 32, sl] + x[160 + 32 * c:192 + 32 * c, sl]) * jnp.broadcast_to(sc[c, pl.ds(t, 1), :], (32, 128))
                g = y if g is None else g + y
            s = jnp.broadcast_to(ss[pl.ds(t, 1), :], (8, 128))
            tot = None
            for j in range(4):
                y = jnp.where(i8 + 8.0 * j == s, g[8 * j:8 * j + 8], 0.0)
                tot = y if tot is None else tot + y
            rows.append(jnp.sum(tot, axis=0, keepdims=True))
        out[pl.ds(pl.multiple_of(base, 8), STEP), :] = jnp.concatenate(rows, 0)
        return 0

    lax.fori_loop(0, SLOOPS, body, 0)


def fwd_att(tab, full, ac, ma, w_tab, alo, ahi, sa, wk, out):
    def body(b, _):
        base = AROWS + b * ASTEP
        h = jnp.concatenate([onehot(ma, base + u, 256) for u in range(ASTEP)], 1)
        x = jnp.dot(tab[...], h, preferred_element_type=F32)
        groups = AROWS // 8 // ALOOPS
        for k in range(groups):
            r0 = pl.ds(pl.multiple_of((b * groups + k) * 8, 8), 8)
            lo = alo[r0, :]
            upper = ahi[r0, :] == 1
            s = sa[r0, :]
            w = [wk[j, r0, :] for j in range(4)]
            acc = [jnp.zeros((8, 128), F32)] * 4
            for r in range(35):
                v = jnp.zeros((8, 128), F32)
                for j in range(4):
                    if 0 <= r - j < 32:
                        v = jnp.where(s == r - j, w[j], v)
                for q in range(4):
                    t = [jnp.take_along_axis(jnp.broadcast_to(full[SE * q + r:SE * q + r + 1, a:a + 128], (8, 128)), lo, axis=1)
                         for a in (0, 128)]
                    acc[q] = acc[q] + v * jnp.where(upper, t[1], t[0])
            t = acc[0] * ac[0, r0, :]
            for q in range(1, 4):
                t = t + acc[q] * ac[q, r0, :]
            out[r0, :] = t
        rows = []
        for u in range(ASTEP):
            t = base + u
            sl = slice(128 * u, 128 * u + 128)
            g = None
            for q in range(4):
                y = (x[SE * q:SE * q + SE, sl] + x[4 * SE + SE * q:4 * SE + SE * q + SE, sl]) * jnp.broadcast_to(ac[q, pl.ds(t, 1), :], (SE, 128))
                g = y if g is None else g + y
            g = g * w_tab[t]
            tot = None
            for j in range(SE // 8):
                y = g[8 * j:8 * j + 8]
                tot = y if tot is None else tot + y
            rows.append(jnp.sum(tot, axis=0, keepdims=True))
        out[pl.ds(pl.multiple_of(base, 8), ASTEP), :] = jnp.concatenate(rows, 0)
        return 0

    lax.fori_loop(0, ALOOPS, body, 0)


def tree(xs):
    while len(xs) > 1:
        xs = [a + b for a, b in zip(xs[::2], xs[1::2])]
    return xs[0]


def drain(ref, sem):
    pltpu.make_async_copy(ref, ref, sem).wait()


def to_seg(me, start):
    for i in (2, 1, 3):
        start(lax.rem(me + i, NG), i)


def ring_hops(d):
    return min(d, 4 - d)


OFFSETS = sorted(((z, x, c) for z in range(4) for x in range(4) for c in range(2) if (z, x, c) != (0, 0, 0)),
                 key=lambda o: (-ring_hops(o[0]) - ring_hops(o[1]), -o[2]))


def star_peers(me):
    z = [lax.rem(lax.div(me, 8) + d, 4) * 8 for d in range(4)]
    x = [lax.rem(lax.div(me, 2) + d, 4) * 2 for d in range(4)]
    c = [lax.rem(me + d, 2) for d in range(2)]
    return [(z[a] + x[b] + c[d], i + 1) for i, (a, b, d) in enumerate(OFFSETS)]


def remote(src, dst, send, recv, si, gi):
    pltpu.make_async_remote_copy(src_ref=src, dst_ref=dst, send_sem=send, recv_sem=recv,
                                 device_id=(si, gi), device_id_type=MESH).start()


def kernel(star_h, knot_h, frac_h, sc_h, ac_h, cc_h, obs_h, caln_h, live,
           xs_h, xa_h, xc_h, r_h,
           star, knot, frac, sc, ac, cc, obs, caln, in_sem,
           ms, ss, ma, sa, lo7, hi6, alo, ahi, wk, w_tab, hc, psh, psl, pat, accs, acca,
           gac, gs, rac, rs, fac, fs, halo_v, halo_r, halo_t, halo_d, halo_u, ahead,
           dac, dst, tac, tax, tst, img_a, img_s, img, res,
           s1v, s1r, s2v, s2r, ls, la, oc,
           send_sem, ar_sem, sc_sem):
    me = lax.axis_index("stars")
    seg = lax.axis_index("seg")
    peers = star_peers(me)

    def to_stars(start):
        for p, i in peers:
            start(p, i)

    up = lax.rem(seg + 1, NG)
    down = lax.rem(seg + NG - 1, NG)

    loads = [pltpu.make_async_copy(a, b, in_sem.at[k]) for k, (a, b) in enumerate(
        ((star_h, star), (knot_h, knot), (frac_h, frac), (obs_h, obs), (caln_h, caln), (ac_h, ac), (cc_h, cc), (sc_h, sc)))]
    for c in loads:
        c.start()

    barrier = pltpu.get_barrier_semaphore()

    def hello_stars(p, i):
        pl.semaphore_signal(barrier, inc=1, device_id=(p, seg), device_id_type=MESH)

    def hello_seg(p, i):
        pl.semaphore_signal(barrier, inc=1, device_id=(me, p), device_id_type=MESH)

    to_stars(hello_stars)
    to_seg(seg, hello_seg)

    for c in loads[:3]:
        c.wait()
    prepare(star, knot, frac, ms, ss, ma, sa, lo7, hi6, alo, ahi, wk, w_tab)
    for c in loads[3:]:
        c.wait()

    mask = jnp.where(iota((128, 128), 0) < live[0], 1.0, 0.0)
    res[...] = obs[...] * mask
    hc[...] = jnp.where(iota((256, 128), 0) == jnp.broadcast_to(caln[...], (256, 128)), 1.0, 0.0).astype(BF)

    lane = iota((8, 128), 1)
    sub = iota((8, 128), 0)
    own = pl.ds(pl.multiple_of(8 * me, 8), 8)
    own_s = pl.ds(pl.multiple_of(40 * seg, 8), 40)

    def column(row, q):
        return jnp.sum(jnp.where((lane == 4 * sub + q) & (sub < 3), jnp.broadcast_to(row, (8, 128)), 0.0), axis=1, keepdims=True)

    def backward(n, val_ref, between):
        v = val_ref[...]
        for q in range(4):
            pat[q] = ac[q] * v
        acca[...] = jnp.zeros_like(acca)
        back_att(0, LOOPS, pat, ma, w_tab, acca)
        hi, lo = split(cc[...] * v)
        cal = jnp.dot(hc[...], hi, preferred_element_type=F32) + jnp.dot(hc[...], lo, preferred_element_type=F32)
        gac[n, 128:256, 0:128] = cal[0:128]
        gac[n, 128:256, 128:256] = cal[128:256]
        row = jnp.zeros((8, 128), F32)
        wide = iota((8, 256), 1)
        for q in range(4):
            x = acca[SE * q:SE * q + SE] + acca[4 * SE + SE * q:4 * SE + SE * q + SE]
            spill = x[32:40]
            over = jnp.sum(jnp.where(wide == 255, spill, 0.0), axis=1, keepdims=True)
            row = row + jnp.where((lane == 4 * sub + q) & (sub < 3), jnp.broadcast_to(over, (8, 128)), 0.0)
            row = row + jnp.where((lane == 16 + 4 * sub + q) & (sub < 3), jnp.broadcast_to(x[0:8, 0:1], (8, 128)), 0.0)
            moved = jnp.where(wide == 0, 0.0, pltpu.roll(spill, 1, 1))
            gac[n, pl.ds(32 * q, 8), :] = x[0:8] + moved
            gac[n, pl.ds(32 * q + 8, 24), :] = x[8:32]
        halo_v[n] = jnp.sum(row, axis=0, keepdims=True)
        halo_r[n, me] = halo_v[n]
        if n == 0:
            pl.semaphore_wait(barrier, NS - 1 + NG - 1)

        def send_halo(p, i):
            remote(halo_v.at[n], halo_r.at[n, me], send_sem.at[n, 0], ar_sem.at[n, 0], p, seg)

        def send_rs(p, i):
            remote(gac.at[n, pl.ds(pl.multiple_of(8 * p, 8), 8)], rac.at[n, pl.ds(8 * (i - 1), 8)],
                   send_sem.at[n, 1], ar_sem.at[n, 1], p, seg)

        to_stars(send_rs)
        to_stars(send_halo)
        between()

        for c in range(5):
            p = sc[c] * v
            h = p.astype(BF).astype(F32)
            psh[c] = h
            psl[c] = p - h
        accs[...] = jnp.zeros_like(accs)
        back_star(0, LOOPS, psh, psl, ms, ss, accs)
        gs[n] = accs[0:160] + accs[160:320]

        def send_rs_star(p, i):
            remote(gs.at[n, pl.ds(pl.multiple_of(40 * p, 8), 40)], rs.at[n, pl.ds(40 * (i - 1), 40)],
                   send_sem.at[n, 2], ar_sem.at[n, 2], me, p)

        to_seg(seg, send_rs_star)

    def reduce_att(n):
        drain(rac.at[n], ar_sem.at[n, 1])
        fac[n, own, :] = tree([gac[n, own, :]] + [rac[n, 8 * i:8 * i + 8, :] for i in range(NS - 1)])

        def send_ag(p, i):
            remote(fac.at[n, own], fac.at[n, own], send_sem.at[n, 4], ar_sem.at[n, 4], p, seg)

        to_stars(send_ag)

        drain(halo_r.at[n, pl.ds(0, NS - 1)], ar_sem.at[n, 0])
        halo_t[n] = tree([halo_r[n, i] for i in range(NS)])
        remote(halo_t.at[n], halo_d.at[n], send_sem.at[n, 3], ar_sem.at[n, 3], me, up)
        remote(halo_t.at[n], halo_u.at[n], send_sem.at[n, 6], ar_sem.at[n, 6], me, down)

    def reduce_star(n):
        drain(rs.at[n], ar_sem.at[n, 2])
        fs[n, own_s, :] = gs[n, own_s, :] + rs[n, 0:40, :] + rs[n, 40:80, :] + rs[n, 80:120, :]

        def send_ag_star(p, i):
            remote(fs.at[n, own_s], fs.at[n, own_s], send_sem.at[n, 5], ar_sem.at[n, 5], me, p)

        to_seg(seg, send_ag_star)

    def from_below(n):
        return jnp.where(seg > 0, halo_d[n], 0.0)

    def first_knots(n, q):
        return jnp.where(iota((8, 256), 1) == 0, jnp.broadcast_to(column(from_below(n), q), (8, 256)), 0.0)

    def halo(n, combine):
        drain(halo_d.at[n], ar_sem.at[n, 3])
        drain(halo_u.at[n], ar_sem.at[n, 6])
        t = pltpu.roll(jnp.broadcast_to(halo_u[n], (8, 128)), 112, 1)[0:1] + halo_t[n]
        ahead[n] = combine(jnp.where(seg < NG - 1, t, 0.0), ahead, slice(None))

    def own_norm(n, combine):
        mine = jnp.where((lax.rem(me, 4) == 0) & (me < 16), 1.0, 0.0)
        a = combine(fac[n, own, :] + mine * first_knots(n, me // 4), dac, own)
        s = combine(fs[n, own_s, :], dst, own_s)
        return lanes(a * a) + lanes(s * s)

    def gather_att(n, combine):
        drain(fac.at[n, pl.ds(0, 248)], ar_sem.at[n, 4])
        parts = []
        for q in range(4):
            a = pl.ds(32 * q, 8)
            b = pl.ds(32 * q + 8, 24)
            x = combine(fac[n, a, :] + first_knots(n, q), dac, a)
            y = combine(fac[n, b, :], dac, b)
            dac[n, a, :] = x
            dac[n, b, :] = y
            nb = jnp.broadcast_to(column(ahead[n], q), (8, 256))
            parts += [x, y, jnp.where(iota((8, 256), 1) == 255, nb, pltpu.roll(x, 255, 1))]
        c = pl.ds(128, 128)
        dac[n, c, :] = combine(fac[n, c, :], dac, c)
        tax[...] = jnp.concatenate(parts, axis=0)
        h, l = split(tax[...])
        tac[0:4 * SE] = h
        tac[4 * SE:8 * SE] = l

    def gather_star(n, combine):
        drain(fs.at[n, pl.ds(0, 120)], ar_sem.at[n, 5])
        x = combine(fs[n], dst, slice(None))
        dst[n] = x
        h, l = split(x)
        tst[0:160] = h
        tst[160:320] = l

    def put_scalar(k, v):
        s1v[k] = v
        s1r[k, me] = v

        def send(p, i):
            remote(s1v.at[k], s1r.at[k, me], sc_sem.at[k, 0], sc_sem.at[k, 1], p, seg)

        to_stars(send)

    def mid_scalar(k):
        drain(s1r.at[k, pl.ds(0, NS - 1)], sc_sem.at[k, 1])
        t = tree([s1r[k, i] for i in range(NS)])
        s2v[k] = t
        s2r[k, seg] = t

        def send(p, i):
            remote(s2v.at[k], s2r.at[k, seg], sc_sem.at[k, 2], sc_sem.at[k, 3], me, p)

        to_seg(seg, send)

    def get_scalar(k):
        drain(s2r.at[k, pl.ds(0, NG - 1)], sc_sem.at[k, 3])
        t = (s2r[k, 0] + s2r[k, 1]) + (s2r[k, 2] + s2r[k, 3])
        return jnp.sum(t, axis=1, keepdims=True)

    def lanes(x):
        t = jnp.sum(x, axis=0, keepdims=True)
        while t.shape[1] > 128:
            h = t.shape[1] // 2
            t = t[:, :h] + t[:, h:]
        return t

    def cal_image(n):
        x = dac[n, pl.ds(128, 128), :]
        x = jnp.concatenate([x[:, 0:128], x[:, 128:256]], axis=0)
        h, l = split(x)
        tn = (((0,), (0,)), ((), ()))
        v = lax.dot_general(hc[...], h, tn, preferred_element_type=F32) + lax.dot_general(hc[...], l, tn, preferred_element_type=F32)
        return cc[...] * v

    def reduce(n, combine):
        reduce_att(n)
        reduce_star(n)
        halo(n, combine)
        put_scalar(2 * n, own_norm(n, combine))

    def forward(n, combine):
        gather_att(n, combine)
        fwd_att(tac, tax, ac, ma, w_tab, alo, ahi, sa, wk, img_a)
        extra = cal_image(n)
        gather_star(n, combine)
        img_a[...] += extra
        mid_scalar(2 * n)
        fwd_star(tst, dst.at[n], sc, ms, ss, lo7, hi6, img_s)
        return (img_a[...] + img_s[...]) * jnp.where(iota((128, 128), 0) < live[0], 1.0, 0.0)

    def lay_out(n):
        x = dac[n, 0:128]
        h = x.astype(BF)
        rest = x - h.astype(F32)
        m = rest.astype(BF)
        l = (rest - m.astype(F32)).astype(BF)
        col = iota((256, 256), 1)
        pick = jnp.where(iota((256, 256), 0) == 4 * (col & 63) + (col >> 6), 1.0, 0.0).astype(BF)
        y = jnp.dot(jnp.concatenate([h, m, l], axis=0), pick, preferred_element_type=F32)
        y = (y[0:128] + y[128:256]) + y[256:384]
        for q in range(4):
            z = y[32 * q:32 * q + 32]
            a, b = z[:, 0:128], z[:, 128:256]
            t = jnp.concatenate([a, pltpu.roll(a, 64, 1), b, pltpu.roll(b, 64, 1)], axis=0).T
            for i in range(64):
                la[n, q:q + 1, 128 * i:128 * i + 128] = t[i:i + 1]
        for c in range(5):
            for i in range(32):
                ls[n, c:c + 1, 256 * i:256 * i + 256] = dst[n, 32 * c + i:32 * c + i + 1]

    def plain(x, ref, sl):
        return x

    backward(0, res, lambda: None)
    reduce(0, plain)
    img[...] = forward(0, plain)
    put_scalar(1, lanes(img[...] * img[...]))
    backward(1, img, lambda: mid_scalar(1))
    gg0 = get_scalar(0)
    alpha0 = gg0 / get_scalar(1)

    def step(x, ref, sl):
        return ref[0, sl] - alpha0 * x

    reduce(1, step)
    lay_out(0)
    img1 = forward(1, step)
    gg1 = get_scalar(2)
    beta = gg1 / gg0
    img1 = img1 + beta * img[...]
    put_scalar(3, lanes(img1 * img1))
    lay_out(1)
    oc[0, 0:128] = dac[0, 128:256, 0:128]
    oc[0, 128:256] = dac[0, 128:256, 128:256]
    oc[1, 0:128] = dac[1, 128:256, 0:128]
    oc[1, 128:256] = dac[1, 128:256, 128:256]
    res[...] = res[...] - alpha0 * img[...]
    img[...] = img1
    for n in range(2):
        drain(halo_r.at[n, pl.ds(0, NS - 1)], send_sem.at[n, 0])
        drain(rac.at[n], send_sem.at[n, 1])
        drain(rs.at[n], send_sem.at[n, 2])
        drain(halo_d.at[n], send_sem.at[n, 3])
        drain(fac.at[n, pl.ds(0, 248)], send_sem.at[n, 4])
        drain(fs.at[n, pl.ds(0, 120)], send_sem.at[n, 5])
        drain(halo_u.at[n], send_sem.at[n, 6])
    mid_scalar(3)
    alpha1 = gg1 / get_scalar(3)
    ab = alpha0 + alpha1 * beta
    res[...] = res[...] - alpha1 * img[...]
    for o in (ls, la, oc):
        o[0] = ab * o[0] + alpha1 * o[1]
    stores = [pltpu.make_async_copy(a, b, in_sem.at[k]) for k, (a, b) in enumerate(
        ((ls.at[0], xs_h), (la.at[0], xa_h), (oc.at[0], xc_h), (res, r_h)))]
    for c in stores:
        c.start()

    for k in range(4):
        drain(s1r.at[k, pl.ds(0, NS - 1)], sc_sem.at[k, 0])
        drain(s2r.at[k, pl.ds(0, NG - 1)], sc_sem.at[k, 2])
    for c in stores:
        c.wait()


def finish(a, b, c, d, ao, bo, co, do, av, bv, cv, dv, sem_in, sem_out):
    loads = [pltpu.make_async_copy(x, y, sem_in.at[k]) for k, (x, y) in enumerate(((a, av), (b, bv), (c, cv), (d, dv)))]
    stores = [pltpu.make_async_copy(x, y, sem_out.at[k]) for k, (x, y) in enumerate(((av, ao), (bv, bo), (cv, co), (dv, do)))]
    for x in loads:
        x.start()
    for x, y in zip(loads, stores):
        x.wait()
        y.start()
    for y in stores:
        y.wait()


def on_device(star, knot, frac, sc, ac, cc, tile_cal, live, obs):
    shape = jax.ShapeDtypeStruct
    T = (128, 128)
    hbm = pl.BlockSpec(memory_space=pl.ANY)
    V = pltpu.VMEM
    sem = pltpu.SemaphoreType.DMA
    outs = [shape((5, 8192), F32), shape((4, 8192), F32), shape((256, 128), F32), shape(T, F32)]
    parts = pl.pallas_call(
        kernel,
        in_specs=[hbm] * 8 + [pl.BlockSpec(memory_space=pltpu.SMEM)],
        out_specs=[hbm] * 4,
        out_shape=outs,
        scratch_shapes=[
            V(T, jnp.int32), V(T, jnp.int32), V(T, F32), V((5,) + T, F32), V((4,) + T, F32), V(T, F32), V(T, F32),
            V((1, 128), jnp.int32), sem((8,)),
            V(T, F32), V(T, F32), V(T, F32), V(T, jnp.int32), V((ROWS, 128), jnp.int32), V((ROWS, 128), jnp.int32), V((AROWS, 128), jnp.int32), V((AROWS, 128), jnp.int32), V((4,) + T, F32), V((128, SE, 128), F32),
            V((256, 128), BF), V((5,) + T, F32), V((5,) + T, F32), V((4,) + T, F32), V((320, 256), F32), V((320, 256), F32),
            V((2, 256, 256), F32), V((2, 160, 256), F32), V((2, 248, 256), F32), V((2, 120, 256), F32),
            V((2, 256, 256), F32), V((2, 160, 256), F32),
            V((2, 1, 128), F32), V((2, NS, 1, 128), F32), V((2, 1, 128), F32), V((2, 1, 128), F32), V((2, 1, 128), F32), V((2, 1, 128), F32),
            V((2, 256, 256), F32), V((2, 160, 256), F32), V((320, 256), BF), V((160, 256), F32), V((320, 256), BF),
            V(T, F32), V(T, F32), V(T, F32), V(T, F32),
            V((4, 1, 128), F32), V((4, NS, 1, 128), F32), V((4, 1, 128), F32), V((4, NG, 1, 128), F32),
            V((2, 5, 8192), F32), V((2, 4, 8192), F32), V((2, 256, 128), F32),
            sem((2, 7)), sem((2, 7)), sem((4, 4)),
        ],
        compiler_params=pltpu.CompilerParams(collective_id=0, has_side_effects=True, vmem_limit_bytes=60 << 20),
        name="solve",
    )(star, knot, frac, sc, ac, cc, obs, tile_cal.reshape(1, 128), live)
    return pl.pallas_call(
        finish,
        in_specs=[hbm] * 4,
        out_specs=[hbm] * 4,
        out_shape=outs,
        scratch_shapes=[V(o.shape, F32) for o in outs] + [sem((4,)), sem((4,))],
        compiler_params=pltpu.CompilerParams(vmem_limit_bytes=60 << 20),
        name="finish",
    )(*parts)


def solution(mesh):
    P = jax.sharding.PartitionSpec
    a = P(("stars", "seg"), None)
    b = P(None, ("stars", "seg"), None)
    c = P(("stars", "seg"))
    return jax.shard_map(on_device, mesh=mesh, in_specs=(a, a, a, b, b, a, c, c, a),
                         out_specs=(P(None, "stars"), P(None, "seg"), P("seg", None), a), check_vma=False)
```
